768 devices in a mesh: cuts: 24 (over x_hi, z), group: 32 (over y, x_lo, core).
Axes of the slice: x: 4 (x_hi: 2, x_lo: 2; x = x_hi * 2 + x_lo), y: 8, z: 12, core: 2. Of those that a mesh axis runs over, the one named last changes fastest.
Arguments:
- radiation: float32 [768, 2, 128, 128], P(('cuts', 'group')), may hold values from -6 to 6
- phases: float32 [768, 16, 128], P(('cuts', 'group')), may hold values from -3.140625 to 3.140625
- energy: float32 [768, 16, 128], P(('cuts', 'group')), may hold values from -5 to 5
- pixels: int32 [768, 16, 128], P(('cuts', 'group')), may hold values from 0 to 16383
- destination: int32 [768, 16], P(('cuts', 'group')), may hold values from 0 to 23, as said below
- propagator: float32 [2, 128, 128], replicated, may hold values from -1 to 1
- transmit: float32 [2, 768], replicated, may hold values from -1 to 1
Outputs:
- radiation_out: float32 [768, 2, 128, 128], P(('cuts', 'group'))
The draws below stay inside these ranges and needn't reach their ends.
Inputs may be any that keep to these rules, and one draw needn't show every extreme that they name: `destination`: the blocks of one slice go to exactly 8 different cuts, 2 blocks to each; in every draw some cut receives 2 blocks from every slice of the same position within a cut.
All inputs are finite; a program needn't handle non-finite values.
Results may differ from the reference program's by a relative error of at most 0.0011.
Values sent between devices are 32-bit elements; how exact they have to be, the bound alone decides.
A program may use at most 32 MiB of HBM per device.

```python
import math
import jax
import jax.numpy as jnp
from jax import lax

GRID = 128
BLOCK = 128
BLOCKS = 16
STEPS = 2
SLICES = 768
SEND_CAP = 2
HOT_CUTS = 4
N_CUTS = 24
N_GROUP = 32


def draw_destination(key, part):
    key_offset, key_score, key_order = jax.random.split(key, 3)
    cut_ids = jnp.arange(N_CUTS, dtype=jnp.int32)
    offset = jax.random.randint(key_offset, (), 0, N_CUTS)
    hot_mask = ((cut_ids - offset) % N_CUTS < HOT_CUTS).astype(jnp.int32)
    base_score = jax.random.randint(key_score, (SLICES, N_CUTS), 0, 1000)
    score = (base_score + 1000 * hot_mask[None, :]) * N_CUTS + cut_ids[None, :]
    ranking = jnp.argsort(-score, axis=1)
    picked = ranking[:, :BLOCKS // SEND_CAP]
    order_key = jax.random.randint(key_order, (SLICES, BLOCKS), 0, 1 << 20) * BLOCKS + jnp.arange(BLOCKS, dtype=jnp.int32)[None, :]
    shuffle = jnp.argsort(order_key, axis=1)
    chosen = jnp.take_along_axis(picked, shuffle // SEND_CAP, axis=1)
    return chosen.astype(jnp.int32)


def draw_propagator(key, part):
    key_real, key_imag = jax.random.split(key, 2)
    amplitude = 0.52 / math.sqrt(GRID)
    real_part = jax.random.uniform(key_real, (GRID, GRID), jnp.float32, -amplitude, amplitude)
    imag_part = jax.random.uniform(key_imag, (GRID, GRID), jnp.float32, -amplitude, amplitude)
    real_part = real_part + 0.8 * jnp.eye(GRID, dtype=jnp.float32)
    return jnp.stack([real_part, imag_part])


def plant(array, rng, smallest, largest):
    longest = array.shape.index(max(array.shape))
    spots = []
    for shift in (0, 1):
        where = [jax.random.randint(jax.random.fold_in(rng, axis), (), 0, length) for axis, length in enumerate(array.shape)]
        where[longest] = (where[longest] + shift) % array.shape[longest]
        spots.append(tuple(where))
    return array.at[spots[0]].set(smallest).at[spots[1]].set(largest)


def levels(stream_key, extent, pieces, low, top_value):
    def one(dim, shards_of):
        heights = jax.random.uniform(jax.random.fold_in(jax.random.fold_in(stream_key, 6), dim), (shards_of,), jnp.float32, low / len(pieces), top_value / len(pieces))
        return jnp.repeat(jnp.exp(heights), extent[dim] // shards_of).reshape((-1,) + (1,) * (len(extent) - dim - 1))

    level = one(*pieces[0])
    for cut in pieces[1:]:
        level = level * one(*cut)
    return level


def centred(rng, dims, width, most, cuts=(), held_as=jnp.bfloat16):
    result = width * jax.random.normal(rng, dims, jnp.float32)
    if cuts:
        result = result * levels(rng, dims, cuts, -0.22, 0.18)
    return jnp.clip(result, -most, most).astype(held_as)


def setup_inputs(seed: int = 0) -> dict:
    streams_of = jax.random.split(jax.random.key(seed), 8)
    return {
        "radiation": centred(streams_of[0], (SLICES, 2, GRID, GRID), 1.0, 6.0, ((0, 768),), jnp.float32),
        "phases": jnp.clip(jax.random.uniform(streams_of[1], (SLICES, BLOCKS, BLOCK), jnp.float32, -3.140625, 3.140625), -3.140625, 3.140625),
        "energy": centred(streams_of[2], (SLICES, BLOCKS, BLOCK), 1.0, 5.0, ((0, 768),), jnp.float32),
        "pixels": plant(jax.random.randint(streams_of[3], (SLICES, BLOCKS, BLOCK), 0, GRID * GRID), jax.random.fold_in(streams_of[3], 1), 0, (GRID * GRID) - 1).astype(jnp.int32),
        "destination": draw_destination(jax.random.fold_in(streams_of[7], 71), 0),
        "propagator": draw_propagator(jax.random.fold_in(streams_of[7], 71), 0),
        "transmit": jnp.clip(jax.random.uniform(streams_of[6], (2, SLICES), jnp.float32, -1.0, 1.0), -1.0, 1.0),
    }


KICK_RATE = 0.5
PHASE_RATE = 1.0
EMIT_RATE = 0.5


def rounded(values):
    low_values = values.astype(jnp.bfloat16)
    low_values = lax.optimization_barrier(low_values)
    return low_values.astype(jnp.float32)


def diffract(real_part, imag_part, propagator):
    highest = lax.Precision.HIGHEST
    left_real = jnp.einsum("ij,sjk->sik", propagator[0], real_part, precision=highest) - jnp.einsum("ij,sjk->sik", propagator[1], imag_part, precision=highest)
    left_imag = jnp.einsum("ij,sjk->sik", propagator[0], imag_part, precision=highest) + jnp.einsum("ij,sjk->sik", propagator[1], real_part, precision=highest)
    out_real = jnp.einsum("sik,lk->sil", left_real, propagator[0], precision=highest) - jnp.einsum("sik,lk->sil", left_imag, propagator[1], precision=highest)
    out_imag = jnp.einsum("sik,lk->sil", left_real, propagator[1], precision=highest) + jnp.einsum("sik,lk->sil", left_imag, propagator[0], precision=highest)
    return out_real, out_imag


def undulate(real_part, imag_part, phases, energy, home, row_index, col_index, propagator):
    real_low = rounded(real_part)
    imag_low = rounded(imag_part)
    read_real = real_low[home, row_index, col_index]
    read_imag = imag_low[home, row_index, col_index]
    energy = energy - KICK_RATE * (read_real * jnp.cos(phases) - read_imag * jnp.sin(phases))
    phases = phases + PHASE_RATE * energy
    weight_real = rounded(jnp.cos(phases))
    weight_imag = rounded(-jnp.sin(phases))
    source_real = jnp.zeros_like(real_part).at[home, row_index, col_index].add(weight_real)
    source_imag = jnp.zeros_like(imag_part).at[home, row_index, col_index].add(weight_imag)
    real_part = real_part + EMIT_RATE * source_real
    imag_part = imag_part + EMIT_RATE * source_imag
    real_part, imag_part = diffract(real_part, imag_part, propagator)
    zero_slice = jnp.zeros_like(real_part[:1])
    real_part = jnp.concatenate([zero_slice, real_part[:-1]], axis=0)
    imag_part = jnp.concatenate([zero_slice, imag_part[:-1]], axis=0)
    return real_part, imag_part, phases, energy


def reference(radiation, phases, energy, pixels, destination, propagator, transmit):
    slice_count = radiation.shape[0]
    grid_size = radiation.shape[-1]
    real_part = radiation[:, 0]
    imag_part = radiation[:, 1]
    flat_phase = phases.reshape(-1)
    flat_energy = energy.reshape(-1)
    flat_pixel = pixels.reshape(-1)
    row_index = (flat_pixel // grid_size).astype(jnp.int32)
    col_index = (flat_pixel % grid_size).astype(jnp.int32)
    slice_ids = jnp.arange(slice_count, dtype=jnp.int32)
    home = jnp.broadcast_to(slice_ids[:, None, None], pixels.shape).reshape(-1)
    for step_index in range(STEPS):
        real_part, imag_part, flat_phase, flat_energy = undulate(real_part, imag_part, flat_phase, flat_energy, home, row_index, col_index, propagator)
    complex_field = real_part + 1j * imag_part
    gain = transmit[0] + 1j * transmit[1]
    filtered = jnp.fft.ifft(jnp.fft.fft(complex_field, axis=0) * gain[:, None, None], axis=0)
    real_part = jnp.real(filtered)
    imag_part = jnp.imag(filtered)
    new_home = destination[:, :, None] * N_GROUP + (slice_ids % N_GROUP)[:, None, None]
    home = jnp.broadcast_to(new_home, pixels.shape).reshape(-1).astype(jnp.int32)
    for step_index in range(STEPS):
        real_part, imag_part, flat_phase, flat_energy = undulate(real_part, imag_part, flat_phase, flat_energy, home, row_index, col_index, propagator)
    return jnp.stack([real_part, imag_part], axis=1)
```

```python
import functools
import math

import jax
import jax.numpy as jnp
from jax import lax
from jax.experimental import pallas as pl
from jax.experimental.pallas import tpu as pltpu
from jax.sharding import PartitionSpec as P

KICK_RATE = 0.5
PHASE_RATE = 1.0
EMIT_RATE = 0.5
F32 = jnp.float32
BF16 = jnp.bfloat16
MESH = pl.DeviceIdType.MESH
ROWS = 8
HALF = 4


def iota(shape, dim):
    return lax.broadcasted_iota(jnp.int32, shape, dim)


def split(x):
    high = x.astype(BF16)
    return high, (x - high.astype(F32)).astype(BF16)


def dot(a, b):
    return jnp.dot(a, b, preferred_element_type=F32)


def dot_nt(a, b):
    return lax.dot_general(a, b, (((1,), (1,)), ((), ())), preferred_element_type=F32)


def dot_exact(a, b):
    return jnp.dot(a, b, precision=lax.Precision.HIGHEST, preferred_element_type=F32)


def turns(product, total):
    whole = jnp.floor((product + 0.5) * (1.0 / total))
    angle = (product - whole * total) * (2.0 * math.pi / total)
    return jnp.cos(angle), jnp.sin(angle)


def stack2(a, b, c, d):
    return jnp.concatenate(
        [jnp.concatenate([a, b], axis=1), jnp.concatenate([c, d], axis=1)], axis=0
    )


def triple(matrix):
    high, low = split(matrix)
    return jnp.concatenate([high, high, low], axis=1)


def apply_triple(packed, data):
    high, low = split(data)
    return dot(packed, jnp.concatenate([high, low, high], axis=0))


def kernel(
    n_cuts, n_group, grid, blocks, width,
    radiation, phases, energy, pixels, destination, propagator, transmit,
    out,
    field, prop_hi, prop_lo, cut_fwd, cut_inv, mid_op,
    slip_a, got_a, slip_p, got_p, slip_b, got_b,
    pix, onehot, read, weight, source,
    send1, recv1, send2, recv2, send3, recv3, send4, recv4, send_e, recv_e,
    send_sems, recv_sems,
):
    c = lax.axis_index("cuts")
    g = lax.axis_index("group")
    total = n_cuts * n_group
    me = c * n_group + g
    n_active = grid // ROWS
    lane = c % 3
    active = lane < 2
    idle_cut = c - lane + 2
    half_group = n_group // 2
    my_active = 2 * (c // 3) + lane
    owner = jnp.where(active, c, c - 2 + g // half_group)
    unit = jnp.where(active, g, n_group + g % half_group)
    units = 2 * n_cuts
    many = 2 * n_cuts
    before = (me + total - 1) % total
    after = (me + 1) % total

    def repeat(count, body):
        def step(i, carry):
            body(i)
            return carry
        lax.fori_loop(0, count, step, 0)

    barrier = pltpu.get_barrier_semaphore()

    def hello(cc, gg):
        pl.semaphore_signal(barrier, inc=1, device_id=(cc, gg), device_id_type=MESH)

    hello(before // n_group, before % n_group)
    hello(after // n_group, after % n_group)
    repeat(n_cuts - 1, lambda i: hello((c + 1 + i) % n_cuts, g))

    @pl.when(active)
    def _():
        repeat(n_group - 1, lambda i: hello(c, (g + 1 + i) % n_group))
        repeat(half_group, lambda i: hello(idle_cut, half_group * lane + i))

    @pl.when(jnp.logical_not(active))
    def _():
        repeat(n_group, lambda i: hello(owner, (g + i) % n_group))

    ahead_group = (g + 3) % n_group
    behind_group = (g + n_group - 3) % n_group
    repeat(n_cuts, lambda i: hello((c + i) % n_cuts, ahead_group))
    repeat(n_cuts, lambda i: hello((c + i) % n_cuts, behind_group))

    def meet():
        greeted = 2 + (n_cuts - 1) + 2 * n_cuts

        @pl.when(active)
        def _():
            pl.semaphore_wait(barrier, greeted + n_group - 1 + half_group)

        @pl.when(jnp.logical_not(active))
        def _():
            pl.semaphore_wait(barrier, greeted + n_group)

    def remote(stage, src, dst, cc, gg):
        return pltpu.make_async_remote_copy(
            src_ref=src, dst_ref=dst, send_sem=send_sems.at[stage], recv_sem=recv_sems.at[stage],
            device_id=(cc, gg), device_id_type=MESH,
        )

    def push(stage, src, dst, cc, gg):
        mine = jnp.logical_and(cc == c, gg == g)

        @pl.when(mine)
        def _():
            pltpu.make_async_copy(src, dst, recv_sems.at[stage]).start()

        @pl.when(jnp.logical_not(mine))
        def _():
            remote(stage, src, dst, cc, gg).start()

    def arrived(stage, ref):
        remote(stage, ref, ref, c, g).wait_recv()

    def sent(stage, ref):
        remote(stage, ref, ref, c, g).wait_send()

    def rows_of(ref, index, count):
        return ref.at[pl.ds(pl.multiple_of(index * count, count), count)]

    def chunk_of(count):
        return 8 if count % 8 == 0 else count

    def mark(count):
        chunk = chunk_of(count)
        def body(i):
            first = pl.multiple_of(i * chunk, chunk)
            cells = pix[pl.ds(first, chunk), :] & (grid - 1)
            hot = [
                (iota((grid, width), 0) == jnp.broadcast_to(cells[b:b + 1], (grid, width))).astype(F32).astype(BF16)
                for b in range(chunk)
            ]
            onehot[i] = jnp.concatenate(hot, axis=1)
        repeat(count // chunk, body)

    def look(count):
        chunk = chunk_of(count)
        low = field[...].astype(BF16)
        shift = grid.bit_length() - 1
        def body(i):
            first = pl.multiple_of(i * chunk, chunk)
            cells = lax.shift_right_arithmetic(pix[pl.ds(first, chunk), :], shift)
            real, imag = [], []
            for pair in range(chunk // 2):
                hot = onehot[i, :, pair * 2 * width:(pair + 1) * 2 * width]
                picked = dot(low, hot)
                for b in range(2):
                    match = iota((grid, width), 0) == jnp.broadcast_to(cells[2 * pair + b:2 * pair + b + 1], (grid, width))
                    part = picked[:, b * width:(b + 1) * width]
                    real.append(jnp.sum(jnp.where(match, part[:grid], 0.0), axis=0, keepdims=True))
                    imag.append(jnp.sum(jnp.where(match, part[grid:], 0.0), axis=0, keepdims=True))
            read[0, pl.ds(first, chunk), :] = jnp.concatenate(real, axis=0)
            read[1, pl.ds(first, chunk), :] = jnp.concatenate(imag, axis=0)
        repeat(count // chunk, body)

    def kick(count, phase, power):
        power = power - KICK_RATE * (read[0, :count] * jnp.cos(phase) - read[1, :count] * jnp.sin(phase))
        phase = phase + PHASE_RATE * power
        weight[0, :count] = jnp.cos(phase)
        weight[1, :count] = -jnp.sin(phase)
        return phase, power

    def deposit(count):
        chunk = chunk_of(count)
        shift = grid.bit_length() - 1
        source[...] = jnp.zeros_like(source)
        def body(i):
            first = pl.multiple_of(i * chunk, chunk)
            cells = lax.shift_right_arithmetic(pix[pl.ds(first, chunk), :], shift)
            real = weight[0, pl.ds(first, chunk), :]
            imag = weight[1, pl.ds(first, chunk), :]
            tops, bottoms = [], []
            for b in range(chunk):
                match = iota((grid, width), 0) == jnp.broadcast_to(cells[b:b + 1], (grid, width))
                tops.append(jnp.where(match, jnp.broadcast_to(real[b:b + 1], (grid, width)), 0.0).astype(BF16))
                bottoms.append(jnp.where(match, jnp.broadcast_to(imag[b:b + 1], (grid, width)), 0.0).astype(BF16))
            spread = jnp.concatenate([jnp.concatenate(tops, axis=1), jnp.concatenate(bottoms, axis=1)], axis=0)
            source[...] += dot_nt(spread, onehot[i])
        repeat(count // chunk, body)

    def diffract(keep):
        emitted = field[...] + EMIT_RATE * source[...]
        high, low = split(emitted)
        both = dot(prop_hi[...], jnp.concatenate([high, low], axis=1))
        left = both[:, :grid] + both[:, grid:] + dot(prop_lo[...], high)
        left = jnp.concatenate([left[:grid], left[grid:]], axis=1)
        high, low = split(left)
        result = dot_nt(high, prop_hi[...]) + dot_nt(low, prop_hi[...]) + dot_nt(high, prop_lo[...])
        return jnp.where(keep, result, 0.0)

    def set_field(result):
        field[:grid] = result[:, :grid]
        field[grid:] = result[:, grid:]

    field[:grid] = radiation[0, 0]
    field[grid:] = radiation[0, 1]
    pix[:blocks] = pixels[0]
    mark(blocks)
    look(blocks)
    phase, power = kick(blocks, phases[0], energy[0])
    slip_a[:blocks] = phase
    slip_a[blocks:2 * blocks] = power
    slip_a[2 * blocks:3 * blocks] = pixels[0].astype(F32)
    slip_a[3 * blocks:] = jnp.zeros_like(slip_a[3 * blocks:])
    slip_a[3 * blocks:3 * blocks + 1, :blocks] = destination[...].astype(F32)

    prop = stack2(propagator[0], -propagator[1], propagator[1], propagator[0])
    high, low = split(prop)
    prop_hi[...] = high
    prop_lo[...] = low
    deposit(blocks)

    meet()
    remote(0, slip_a, got_a, before // n_group, before % n_group).start()

    set_field(diffract(me != total - 1))
    shape = (n_cuts, n_cuts)
    g_real = g.astype(F32)
    cos, sin = turns((iota(shape, 1).astype(F32) * n_group + g_real) * iota(shape, 0).astype(F32), total)
    cut_fwd[...] = triple(stack2(cos, sin, -sin, cos))
    cos, sin = turns((iota(shape, 0).astype(F32) * n_group + g_real) * iota(shape, 1).astype(F32), total)
    cut_inv[...] = triple(stack2(cos, -sin, sin, cos))
    first_freq = unit // 2
    shape = (n_group, total)
    chosen = iota(shape, 1) == first_freq + n_cuts * iota(shape, 0)
    gain_real = jnp.sum(jnp.where(chosen, jnp.broadcast_to(transmit[0:1], shape), 0.0), axis=1, keepdims=True)
    gain_imag = jnp.sum(jnp.where(chosen, jnp.broadcast_to(transmit[1:2], shape), 0.0), axis=1, keepdims=True)
    shape = (n_group, n_group)
    lag_cos, lag_sin = turns((first_freq.astype(F32) + n_cuts * iota(shape, 0).astype(F32)) * 4.0, total)
    scale = 1.0 / total
    turn_real = (gain_real * lag_cos + gain_imag * lag_sin) * scale
    turn_imag = (gain_imag * lag_cos - gain_real * lag_sin) * scale
    cos, sin = turns(iota(shape, 0).astype(F32) * iota(shape, 1).astype(F32), n_group)
    shaped_real = turn_real * cos + turn_imag * sin
    shaped_imag = turn_imag * cos - turn_real * sin
    mid_op[...] = triple(dot_exact(
        stack2(cos, -sin, sin, cos), stack2(shaped_real, -shaped_imag, shaped_imag, shaped_real)
    ))

    arrived(0, got_a)
    pix[:blocks] = got_a[2 * blocks:3 * blocks].astype(jnp.int32)
    mark(blocks)
    look(blocks)
    phase, power = kick(blocks, got_a[:blocks], got_a[blocks:2 * blocks])
    deposit(blocks)
    result = diffract(me != total - 2)
    for a in range(n_active):
        send1[a * 2 * ROWS:a * 2 * ROWS + ROWS] = result[a * ROWS:(a + 1) * ROWS, :grid]
        send1[a * 2 * ROWS + ROWS:(a + 1) * 2 * ROWS] = result[a * ROWS:(a + 1) * ROWS, grid:]

    def to_active(i):
        a = (i + my_active) % n_active
        push(1, rows_of(send1, a, 2 * ROWS), rows_of(recv1, c, 2 * ROWS), 3 * (a // 2) + a % 2, g)
    repeat(n_active, to_active)

    target = got_a[3 * blocks:3 * blocks + 1, :blocks]
    square = (blocks, blocks)
    wide = jnp.broadcast_to(target, square)
    tall = jnp.sum(jnp.where(iota(square, 0) == iota(square, 1), wide, 0.0), axis=1, keepdims=True)
    same = jnp.logical_and(jnp.broadcast_to(tall, square) == wide, iota(square, 0) < iota(square, 1))
    rank = jnp.sum(jnp.where(same, 1.0, 0.0), axis=0, keepdims=True)
    payload = jnp.concatenate([phase, power, got_a[2 * blocks:3 * blocks] + 1.0], axis=1)
    shape = (n_cuts, blocks)
    goes = jnp.broadcast_to(target, shape) == iota(shape, 0).astype(F32)
    send_e[...] = jnp.zeros_like(send_e)
    for slot in range(2):
        pick = jnp.logical_and(goes, jnp.broadcast_to(rank, shape) == float(slot))
        moved = dot_exact(jnp.where(pick, 1.0, 0.0), payload)
        for part in range(3):
            send_e[pl.ds(slot * 3 + part, n_cuts, stride=8), :] = moved[:, part * width:(part + 1) * width]
    carry_cut = jnp.where(jnp.logical_and(g >= n_group - 3, g <= n_group - 2), 1, 0)

    def to_cut(i):
        k = (i + c) % n_cuts
        push(5, rows_of(send_e, k, 8), rows_of(recv_e, c, 8), (k + carry_cut) % n_cuts, ahead_group)

    @pl.when(active)
    def _():
        arrived(1, recv1)
        real = [recv1[pl.ds(j, n_cuts, stride=2 * ROWS), :] for j in range(ROWS)]
        imag = [recv1[pl.ds(ROWS + j, n_cuts, stride=2 * ROWS), :] for j in range(ROWS)]
        data = jnp.concatenate([jnp.concatenate(real, axis=1), jnp.concatenate(imag, axis=1)], axis=0)
        spec = apply_triple(cut_fwd[...], data)
        for j in range(ROWS):
            at = (j // HALF) * 2 * HALF + j % HALF
            send2[pl.ds(at, n_cuts, stride=2 * ROWS), :] = spec[:n_cuts, j * grid:(j + 1) * grid]
            send2[pl.ds(at + HALF, n_cuts, stride=2 * ROWS), :] = spec[n_cuts:, j * grid:(j + 1) * grid]

        def to_idle(i):
            push(2, rows_of(send2, n_group + i, 8), rows_of(recv2, g, 8), idle_cut, half_group * lane + i)
        def to_member(i):
            m = (i + g) % n_group
            push(2, rows_of(send2, m, 8), rows_of(recv2, g, 8), c, m)
        repeat(half_group, to_idle)
        repeat(n_group, to_member)
        repeat(n_cuts, to_cut)

    arrived(2, recv2)
    real = [recv2[pl.ds(j, n_group, stride=8), :] for j in range(HALF)]
    imag = [recv2[pl.ds(HALF + j, n_group, stride=8), :] for j in range(HALF)]
    data = jnp.concatenate([jnp.concatenate(real, axis=1), jnp.concatenate(imag, axis=1)], axis=0)
    shaped = apply_triple(mid_op[...], data)
    for j in range(HALF):
        send3[pl.ds(j, n_group, stride=8), :] = shaped[:n_group, j * grid:(j + 1) * grid]
        send3[pl.ds(HALF + j, n_group, stride=8), :] = shaped[n_group:, j * grid:(j + 1) * grid]

    def to_owner(i):
        m = (i + g) % n_group
        push(3, rows_of(send3, m, 8), rows_of(recv3, unit, 8), owner, m)
    repeat(n_group, to_owner)

    @pl.when(jnp.logical_not(active))
    def _():
        repeat(n_cuts, to_cut)

    @pl.when(active)
    def _():
        arrived(3, recv3)
        real, imag = [], []
        for j in range(ROWS):
            at = (j // HALF) * 2 * HALF + j % HALF
            real.append(recv3[pl.ds(at, n_cuts, stride=2 * ROWS), :])
            imag.append(recv3[pl.ds(at + HALF, n_cuts, stride=2 * ROWS), :])
        data = jnp.concatenate([jnp.concatenate(real, axis=1), jnp.concatenate(imag, axis=1)], axis=0)
        back = apply_triple(cut_inv[...], data)
        for j in range(ROWS):
            send4[pl.ds(j, n_cuts, stride=2 * ROWS), :] = back[:n_cuts, j * grid:(j + 1) * grid]
            send4[pl.ds(ROWS + j, n_cuts, stride=2 * ROWS), :] = back[n_cuts:, j * grid:(j + 1) * grid]

        def to_slice(i):
            k = (i + c) % n_cuts
            push(4, rows_of(send4, k, 2 * ROWS), rows_of(recv4, my_active, 2 * ROWS), k, g)
        repeat(n_cuts, to_slice)

    arrived(5, recv_e)
    def pieces(part):
        return jnp.concatenate(
            [recv_e[pl.ds(part, n_cuts, stride=8), :], recv_e[pl.ds(3 + part, n_cuts, stride=8), :]], axis=0
        )
    cells = pieces(2)
    slip_p[...] = cells
    remote(6, slip_p, got_p, before // n_group, before % n_group).start()
    pix[...] = (cells + 0.25).astype(jnp.int32) - 1
    mark(many)
    arrived(4, recv4)
    for a in range(n_active):
        field[a * ROWS:(a + 1) * ROWS] = recv4[a * 2 * ROWS:a * 2 * ROWS + ROWS]
        field[grid + a * ROWS:grid + (a + 1) * ROWS] = recv4[a * 2 * ROWS + ROWS:(a + 1) * 2 * ROWS]

    look(many)
    phase, power = kick(many, pieces(0), pieces(1))
    slip_b[:many] = phase
    slip_b[many:] = power
    remote(7, slip_b, got_b, before // n_group, before % n_group).start()
    deposit(many)
    set_field(diffract(me != 1))

    arrived(6, got_p)
    pix[...] = (got_p[...] + 0.25).astype(jnp.int32) - 1
    mark(many)
    look(many)
    arrived(7, got_b)
    kick(many, got_b[:many], got_b[many:])
    deposit(many)
    result = diffract(me != 0)
    out[0, 0] = result[:, :grid]
    out[0, 1] = result[:, grid:]

    sent(0, slip_a)
    sent(6, slip_p)
    sent(7, slip_b)
    sent(5, send_e)

    @pl.when(active)
    def _():
        sent(1, send1.at[pl.ds(0, (n_active - 1) * 2 * ROWS)])
        sent(2, send2.at[pl.ds(0, (units - 1) * 8)])
        sent(3, send3.at[pl.ds(0, (n_group - 1) * 8)])
        sent(4, send4.at[pl.ds(0, (n_cuts - 1) * 2 * ROWS)])

    @pl.when(jnp.logical_not(active))
    def _():
        sent(1, send1)
        sent(3, send3)


def on_device(n_cuts, n_group, radiation, phases, energy, pixels, destination, propagator, transmit):
    grid = radiation.shape[-1]
    blocks, width = phases.shape[1:]
    many = 2 * n_cuts
    chunk = 8 if many % 8 == 0 else many
    marks = (max(blocks, many) // chunk, grid, chunk * width)
    if blocks % 8 or many % 8:
        marks = (1, grid, many * width)
    n_active = grid // ROWS
    vmem = lambda shape, kind=F32: pltpu.VMEM(shape, kind)
    sizes = [n_active * 2 * ROWS, n_cuts * 2 * ROWS, n_cuts * 16, n_group * 8,
             n_group * 8, n_cuts * 16, n_cuts * 2 * ROWS, n_active * 2 * ROWS]
    scratch = [
        vmem((2 * grid, grid)),
        vmem((2 * grid, 2 * grid), BF16),
        vmem((2 * grid, 2 * grid), BF16),
        vmem((2 * n_cuts, 6 * n_cuts), BF16),
        vmem((2 * n_cuts, 6 * n_cuts), BF16),
        vmem((2 * n_group, 6 * n_group), BF16),
        vmem((3 * blocks + 8, width)),
        vmem((3 * blocks + 8, width)),
        vmem((many, width)),
        vmem((many, width)),
        vmem((2 * many, width)),
        vmem((2 * many, width)),
        vmem((many, width), jnp.int32),
        vmem(marks, BF16),
        vmem((2, many, width)),
        vmem((2, many, width)),
        vmem((2 * grid, grid)),
    ]
    scratch += [vmem((rows, grid)) for rows in sizes]
    scratch += [vmem((n_cuts * 8, width)), vmem((n_cuts * 8, width))]
    scratch += [pltpu.SemaphoreType.DMA((8,)), pltpu.SemaphoreType.DMA((8,))]
    return pl.pallas_call(
        functools.partial(kernel, n_cuts, n_group, grid, blocks, width),
        out_shape=jax.ShapeDtypeStruct(radiation.shape, F32),
        in_specs=[pl.BlockSpec(memory_space=pltpu.VMEM)] * 7,
        out_specs=pl.BlockSpec(memory_space=pltpu.VMEM),
        scratch_shapes=scratch,
        compiler_params=pltpu.CompilerParams(collective_id=0, has_side_effects=True),
    )(radiation, phases, energy, pixels, destination, propagator, transmit)


def solution(mesh):
    sizes = dict(mesh.shape)
    return jax.shard_map(
        functools.partial(on_device, sizes["cuts"], sizes["group"]),
        mesh=mesh,
        in_specs=(
            P(("cuts", "group"), None, None, None),
            P(("cuts", "group"), None, None),
            P(("cuts", "group"), None, None),
            P(("cuts", "group"), None, None),
            P(("cuts", "group"), None),
            P(),
            P(),
        ),
        out_specs=P(("cuts", "group"), None, None, None),
        check_vma=False,
    )
```

```python
import contextlib
import functools
import math

import jax
import jax.numpy as jnp
from jax import lax
from jax.experimental import pallas as pl
from jax.experimental.pallas import tpu as pltpu
from jax.sharding import PartitionSpec as P

KICK_RATE = 0.5
PHASE_RATE = 1.0
EMIT_RATE = 0.5
F32 = jnp.float32
BF16 = jnp.bfloat16
MESH = pl.DeviceIdType.MESH
ROWS = 8
HALF = 4


def tag(name):
    return contextlib.nullcontext()


def iota(shape, dim):
    return lax.broadcasted_iota(jnp.int32, shape, dim)


def split(x):
    high = x.astype(BF16)
    return high, (x - high.astype(F32)).astype(BF16)


def dot(a, b):
    return jnp.dot(a, b, preferred_element_type=F32)


def dot_nt(a, b):
    return lax.dot_general(a, b, (((1,), (1,)), ((), ())), preferred_element_type=F32)


def dot_exact(a, b):
    return jnp.dot(a, b, precision=lax.Precision.HIGHEST, preferred_element_type=F32)


def turns(product, total):
    whole = jnp.floor((product + 0.5) * (1.0 / total))
    angle = (product - whole * total) * (2.0 * math.pi / total)
    return jnp.cos(angle), jnp.sin(angle)


def stack2(a, b, c, d):
    return jnp.concatenate(
        [jnp.concatenate([a, b], axis=1), jnp.concatenate([c, d], axis=1)], axis=0
    )


def triple(matrix):
    high, low = split(matrix)
    return jnp.concatenate([high, high, low], axis=1)


def apply_triple(packed, data):
    high, low = split(data)
    return dot(packed, jnp.concatenate([high, low, high], axis=0))


def kernel(
    n_cuts, n_group, grid, blocks, width,
    radiation, phases, energy, pixels, destination, propagator, transmit,
    out,
    phase_in, power_in, pixel_in, target_in, prop_in, gain_in, result_out,
    field, prop_hi, prop_lo, cut_fwd, cut_inv, mid_op,
    slip_a, got_a, slip_e, slip_p, got_p, slip_b, got_b,
    hot_now, hot_next, row_now, row_next, read, weight, source,
    send1, recv1, send2, recv2, send3, recv3, send4, recv4, send_e, recv_e,
    load_sems, send_sems, recv_sems,
):
    c = lax.axis_index("cuts")
    g = lax.axis_index("group")
    total = n_cuts * n_group
    me = c * n_group + g
    n_active = grid // ROWS
    lane = c % 3
    active = lane != 1
    idle = jnp.logical_not(active)
    side = lane // 2
    idle_cut = c - lane + 1
    half_group = n_group // 2
    my_active = 2 * (c // 3) + side
    owner = jnp.where(active, c, c - 1 + 2 * (g // half_group))
    unit = jnp.where(active, g, n_group + g % half_group)
    many = 2 * n_cuts

    def device(offset):
        other = (me + total + offset) % total
        return other // n_group, other % n_group

    def repeat(count, body):
        def step(i, carry):
            body(i)
            return carry
        lax.fori_loop(0, count, step, 0)

    loads = [
        pltpu.make_async_copy(src, dst, load_sems.at[i])
        for i, (src, dst) in enumerate([
            (pixels.at[0], pixel_in), (radiation.at[0, 0], field.at[pl.ds(0, grid)]),
            (radiation.at[0, 1], field.at[pl.ds(grid, grid)]), (phases.at[0], phase_in),
            (energy.at[0], power_in), (destination, target_in), (propagator, prop_in), (transmit, gain_in),
        ])
    ]
    for load in loads:
        load.start()
    barrier = pltpu.get_barrier_semaphore()

    def hello(cc, gg):
        pl.semaphore_signal(barrier, inc=1, device_id=(cc, gg), device_id_type=MESH)

    for offset in (-1, 1, -3, 3):
        hello(*device(offset))
    repeat(n_cuts - 1, lambda i: hello((c + 1 + i) % n_cuts, g))

    @pl.when(active)
    def _():
        repeat(n_group - 1, lambda i: hello(c, (g + 1 + i) % n_group))
        repeat(half_group, lambda i: hello(idle_cut, half_group * side + i))

    @pl.when(idle)
    def _():
        repeat(n_group, lambda i: hello(owner, (g + i) % n_group))

    def meet():
        greeted = 4 + n_cuts - 1

        @pl.when(active)
        def _():
            pl.semaphore_wait(barrier, greeted + n_group - 1 + half_group)

        @pl.when(idle)
        def _():
            pl.semaphore_wait(barrier, greeted + n_group)

    def remote(stage, src, dst, cc, gg):
        return pltpu.make_async_remote_copy(
            src_ref=src, dst_ref=dst, send_sem=send_sems.at[stage], recv_sem=recv_sems.at[stage],
            device_id=(cc, gg), device_id_type=MESH,
        )

    def push(stage, src, dst, cc, gg):
        mine = jnp.logical_and(cc == c, gg == g)

        @pl.when(mine)
        def _():
            pltpu.make_async_copy(src, dst, recv_sems.at[stage]).start()

        @pl.when(jnp.logical_not(mine))
        def _():
            remote(stage, src, dst, cc, gg).start()

    def arrived(stage, ref):
        with tag("wait%d" % stage):
            remote(stage, ref, ref, c, g).wait_recv()

    def sent(stage, ref):
        remote(stage, ref, ref, c, g).wait_send()

    def tile(ref, index):
        return ref.at[pl.ds(pl.multiple_of(index * 8, 8), 8)]

    shift = grid.bit_length()
    pairs = grid // 2
    places = 2 * grid

    def chunk_of(count):
        return 8 if count % 8 == 0 else count

    def mark(count, cells, hot, rows):
        chunk = chunk_of(count)
        for i in range(count // chunk):
            part = cells[i * chunk:(i + 1) * chunk]
            rows[i * chunk:(i + 1) * chunk] = lax.shift_right_arithmetic(part, shift)
            place = part & (places - 1)
            for b in range(chunk):
                match = iota((places, width), 0) == jnp.broadcast_to(place[b:b + 1], (places, width))
                hot[i, :, b * width:(b + 1) * width] = jnp.where(match, 1.0, 0.0).astype(BF16)

    def look(count, hot, rows):
        chunk = chunk_of(count)
        low = jnp.concatenate([field[pl.ds(0, grid, stride=2), :], field[pl.ds(1, grid, stride=2), :]], axis=1).astype(BF16)
        def body(i):
            first = pl.multiple_of(i * chunk, chunk)
            at = rows[pl.ds(first, chunk), :]
            real, imag = [], []
            for two in range(chunk // 2):
                picked = dot(low, hot[i, :, two * 2 * width:(two + 1) * 2 * width])
                for b in range(2):
                    match = iota((pairs, width), 0) == jnp.broadcast_to(at[2 * two + b:2 * two + b + 1], (pairs, width))
                    part = picked[:, b * width:(b + 1) * width]
                    real.append(jnp.sum(jnp.where(match, part[:pairs], 0.0), axis=0, keepdims=True))
                    imag.append(jnp.sum(jnp.where(match, part[pairs:], 0.0), axis=0, keepdims=True))
            read[0, pl.ds(first, chunk), :] = jnp.concatenate(real, axis=0)
            read[1, pl.ds(first, chunk), :] = jnp.concatenate(imag, axis=0)
        repeat(count // chunk, body)

    def kick(count, phase, power, cos, sin):
        power = power - KICK_RATE * (read[0, :count] * cos - read[1, :count] * sin)
        phase = phase + PHASE_RATE * power
        weight[0, :count] = jnp.cos(phase)
        weight[1, :count] = -jnp.sin(phase)
        return phase, power

    def deposit(count, hot, rows):
        chunk = chunk_of(count)
        source[...] = jnp.zeros_like(source)
        def body(i):
            first = pl.multiple_of(i * chunk, chunk)
            at = rows[pl.ds(first, chunk), :]
            real = weight[0, pl.ds(first, chunk), :]
            imag = weight[1, pl.ds(first, chunk), :]
            tops, bottoms = [], []
            shape = (pairs, width)
            for b in range(chunk):
                match = iota(shape, 0) == jnp.broadcast_to(at[b:b + 1], shape)
                tops.append(jnp.where(match, jnp.broadcast_to(real[b:b + 1], shape), 0.0).astype(BF16))
                bottoms.append(jnp.where(match, jnp.broadcast_to(imag[b:b + 1], shape), 0.0).astype(BF16))
            spread = jnp.concatenate([jnp.concatenate(tops, axis=1), jnp.concatenate(bottoms, axis=1)], axis=0)
            source[...] += dot_nt(spread, hot[i])
        repeat(count // chunk, body)

    def emit():
        field[pl.ds(0, grid, stride=2), :] = field[pl.ds(0, grid, stride=2), :] + EMIT_RATE * source[:, :grid]
        field[pl.ds(1, grid, stride=2), :] = field[pl.ds(1, grid, stride=2), :] + EMIT_RATE * source[:, grid:]

    def diffract(keep):
        emit()
        high, low = split(field[...])
        both = dot(prop_hi[...], jnp.concatenate([high, low], axis=1))
        left = both[:, :grid] + both[:, grid:] + dot(prop_lo[...], high)
        left = jnp.concatenate([left[:grid], left[grid:]], axis=1)
        high, low = split(left)
        result = dot_nt(high, prop_hi[...]) + dot_nt(low, prop_hi[...]) + dot_nt(high, prop_lo[...])
        return jnp.where(keep, result, 0.0)

    def set_field(result):
        field[:grid] = result[:, :grid]
        field[grid:] = result[:, grid:]

    loads[0].wait()
    mark(blocks, pixel_in[...], hot_now, row_now)
    for load in loads[1:]:
        load.wait()
    look(blocks, hot_now, row_now)
    phase = phase_in[...]
    phase, power = kick(blocks, phase, power_in[...], jnp.cos(phase), jnp.sin(phase))
    slip_a[:blocks] = phase
    slip_a[blocks:2 * blocks] = power
    slip_a[2 * blocks:3 * blocks] = pixel_in[...].astype(F32)
    slip_a[3 * blocks:] = jnp.zeros_like(slip_a[3 * blocks:])
    slip_a[3 * blocks:3 * blocks + 1, :blocks] = target_in[...].astype(F32)
    with tag("meet"):
        meet()
    remote(0, slip_a, got_a, *device(-1)).start()
    prop = stack2(prop_in[0], -prop_in[1], prop_in[1], prop_in[0])
    high, low = split(prop)
    prop_hi[...] = high
    prop_lo[...] = low
    deposit(blocks, hot_now, row_now)
    set_field(diffract(me != total - 1))

    arrived(0, got_a)
    mark(blocks, got_a[2 * blocks:3 * blocks].astype(jnp.int32), hot_now, row_now)
    look(blocks, hot_now, row_now)
    phase = got_a[:blocks]
    phase, power = kick(blocks, phase, got_a[blocks:2 * blocks], jnp.cos(phase), jnp.sin(phase))
    deposit(blocks, hot_now, row_now)
    result = diffract(me != total - 2)
    for a in range(n_active):
        for h in range(2):
            at = a * ROWS + h * HALF
            send1[h, a * 8:a * 8 + HALF] = result[at:at + HALF, :grid]
            send1[h, a * 8 + HALF:(a + 1) * 8] = result[at:at + HALF, grid:]

    for h in range(2):
        def to_active(i):
            a = (i + my_active) % n_active
            push(1 + h, tile(send1.at[h], a), tile(recv1.at[h], c), 3 * (a // 2) + 2 * (a % 2), g)
        repeat(n_active, to_active)

    target = got_a[3 * blocks:3 * blocks + 1, :blocks]
    square = (blocks, blocks)
    wide = jnp.broadcast_to(target, square)
    tall = jnp.sum(jnp.where(iota(square, 0) == iota(square, 1), wide, 0.0), axis=1, keepdims=True)
    same = jnp.logical_and(jnp.broadcast_to(tall, square) == wide, iota(square, 0) < iota(square, 1))
    rank = jnp.sum(jnp.where(same, 1.0, 0.0), axis=0, keepdims=True)
    payload = jnp.concatenate([phase, power, got_a[2 * blocks:3 * blocks] + 1.0], axis=1)
    shape = (n_cuts, blocks)
    goes = jnp.broadcast_to(target, shape) == iota(shape, 0).astype(F32)
    send_e[...] = jnp.zeros_like(send_e)
    for slot in range(2):
        pick = jnp.logical_and(goes, jnp.broadcast_to(rank, shape) == float(slot))
        moved = dot_exact(jnp.where(pick, 1.0, 0.0), payload)
        for part in range(3):
            send_e[pl.ds(slot * 3 + part, n_cuts, stride=8), :] = moved[:, part * width:(part + 1) * width]
    borrow = jnp.where(g == n_group - 1, n_cuts - 1, n_cuts)

    def to_cut(i):
        k = (i + c) % n_cuts
        push(9, tile(send_e, k), tile(recv_e, c), (k + borrow) % n_cuts, g)

    shape = (n_cuts, n_cuts)
    g_real = g.astype(F32)
    cos, sin = turns((iota(shape, 1).astype(F32) * n_group + g_real) * iota(shape, 0).astype(F32), total)
    cut_fwd[...] = triple(stack2(cos, sin, -sin, cos))
    cos, sin = turns((iota(shape, 0).astype(F32) * n_group + g_real) * iota(shape, 1).astype(F32), total)
    cut_inv[...] = triple(stack2(cos, -sin, sin, cos))
    first_freq = unit // 2
    shape = (n_group, total)
    chosen = iota(shape, 1) == first_freq + n_cuts * iota(shape, 0)
    gain_real = jnp.sum(jnp.where(chosen, jnp.broadcast_to(gain_in[0:1], shape), 0.0), axis=1, keepdims=True)
    gain_imag = jnp.sum(jnp.where(chosen, jnp.broadcast_to(gain_in[1:2], shape), 0.0), axis=1, keepdims=True)
    shape = (n_group, n_group)
    lag_cos, lag_sin = turns((first_freq.astype(F32) + n_cuts * iota(shape, 0).astype(F32)) * 4.0, total)
    scale = 1.0 / total
    turn_real = (gain_real * lag_cos + gain_imag * lag_sin) * scale
    turn_imag = (gain_imag * lag_cos - gain_real * lag_sin) * scale
    cos, sin = turns(iota(shape, 0).astype(F32) * iota(shape, 1).astype(F32), n_group)
    shaped_real = turn_real * cos + turn_imag * sin
    shaped_imag = turn_imag * cos - turn_real * sin
    mid_op[...] = triple(dot_exact(
        stack2(cos, -sin, sin, cos), stack2(shaped_real, -shaped_imag, shaped_imag, shaped_real)
    ))

    def apply(operator, count, source_ref, target_ref):
        real = [source_ref[pl.ds(j, count, stride=8), :] for j in range(HALF)]
        imag = [source_ref[pl.ds(HALF + j, count, stride=8), :] for j in range(HALF)]
        data = jnp.concatenate([jnp.concatenate(real, axis=1), jnp.concatenate(imag, axis=1)], axis=0)
        done = apply_triple(operator[...], data)
        for j in range(HALF):
            target_ref[pl.ds(j, count, stride=8), :] = done[:count, j * grid:(j + 1) * grid]
            target_ref[pl.ds(HALF + j, count, stride=8), :] = done[count:, j * grid:(j + 1) * grid]

    @pl.when(active)
    def _():
        for h in range(2):
            arrived(1 + h, recv1.at[h])
            with tag("fwd%d" % h):
                apply(cut_fwd, n_cuts, recv1.at[h], send2.at[h])
            def to_unit(i):
                freq = (i + (3 * g) // 4) % n_cuts
                u = 2 * freq + h
                own = u < n_group
                push(
                    3, tile(send2.at[h], freq), tile(recv2, g),
                    jnp.where(own, c, idle_cut), jnp.where(own, u, half_group * side + u - n_group),
                )
            with tag("send2%d" % h):
                repeat(n_cuts, to_unit)
        with tag("sende"):
            repeat(n_cuts, to_cut)

    arrived(3, recv2)
    with tag("mid"):
        apply(mid_op, n_group, recv2, send3)

    for h in range(2):
        @pl.when(unit % 2 == h)
        def _():
            def to_owner(i):
                m = (i + g) % n_group
                push(4 + h, tile(send3, m), tile(recv3.at[h], unit // 2), owner, m)
            with tag("send3"):
                repeat(n_group, to_owner)

    @pl.when(idle)
    def _():
        with tag("sende"):
            repeat(n_cuts, to_cut)

    @pl.when(active)
    def _():
        for h in range(2):
            arrived(4 + h, recv3.at[h])
            with tag("inv%d" % h):
                apply(cut_inv, n_cuts, recv3.at[h], send4.at[h])
            def to_slice(i):
                k = (i + c) % n_cuts
                push(6 + h, tile(send4.at[h], k), tile(recv4.at[h], my_active), k, g)
            with tag("send4%d" % h):
                repeat(n_cuts, to_slice)

    arrived(9, recv_e)
    remote(10, recv_e, slip_e, *device(3)).start()
    arrived(10, slip_e)

    def pieces(part):
        return jnp.concatenate(
            [slip_e[pl.ds(part, n_cuts, stride=8), :], slip_e[pl.ds(3 + part, n_cuts, stride=8), :]], axis=0
        )

    def cells_of(value):
        return (value + 0.25).astype(jnp.int32) - 1

    cells = pieces(2)
    slip_p[...] = cells
    remote(11, slip_p, got_p, *device(-1)).start()
    with tag("mark3"):
        mark(many, cells_of(cells), hot_now, row_now)
    phase = pieces(0)
    cos, sin = jnp.cos(phase), jnp.sin(phase)
    arrived(11, got_p)
    with tag("mark4"):
        mark(many, cells_of(got_p[...]), hot_next, row_next)
    for h in range(2):
        arrived(6 + h, recv4.at[h])
        for a in range(n_active):
            at = a * ROWS + h * HALF
            field[at:at + HALF] = recv4[h, a * 8:a * 8 + HALF]
            field[grid + at:grid + at + HALF] = recv4[h, a * 8 + HALF:(a + 1) * 8]

    with tag("look3"):
        look(many, hot_now, row_now)
    with tag("kick3"):
        phase, power = kick(many, phase, pieces(1), cos, sin)
        slip_b[:many] = phase
        slip_b[many:] = power
    remote(12, slip_b, got_b, *device(-1)).start()
    with tag("deposit3"):
        deposit(many, hot_now, row_now)
    with tag("diffract3"):
        set_field(diffract(me != 1))

    with tag("look4"):
        look(many, hot_next, row_next)
    arrived(12, got_b)
    with tag("kick4"):
        phase = got_b[:many]
        kick(many, phase, got_b[many:], jnp.cos(phase), jnp.sin(phase))
    with tag("deposit4"):
        deposit(many, hot_next, row_next)
    with tag("diffract4"):
        result = diffract(me != 0)
        result_out[0] = result[:, :grid]
        result_out[1] = result[:, grid:]
    store = pltpu.make_async_copy(result_out, out.at[0], load_sems.at[0])
    store.start()

    sent(0, slip_a)
    sent(9, send_e.at[pl.ds(0, (n_cuts - 1) * 8)])
    sent(10, recv_e)
    sent(11, slip_p)
    sent(12, slip_b)

    @pl.when(active)
    def _():
        for h in range(2):
            sent(1 + h, send1.at[h, pl.ds(0, (n_active - 1) * 8)])
            sent(6 + h, send4.at[h, pl.ds(0, (n_cuts - 1) * 8)])
        for h in range(2):
            @pl.when(unit % 2 == h)
            def _():
                sent(4 + h, send3.at[pl.ds(0, (n_group - 1) * 8)])
        sent(3, send2.at[0])
        sent(3, send2.at[1, pl.ds(0, (n_cuts - 1) * 8)])

    @pl.when(idle)
    def _():
        for h in range(2):
            sent(1 + h, send1.at[h])
            @pl.when(unit % 2 == h)
            def _():
                sent(4 + h, send3)
    store.wait()


def on_device(n_cuts, n_group, radiation, phases, energy, pixels, destination, propagator, transmit):
    grid = radiation.shape[-1]
    blocks, width = phases.shape[1:]
    many = 2 * n_cuts
    chunk = 8 if many % 8 == 0 else many
    marks = (many // chunk, 2 * grid, chunk * width)
    n_active = grid // ROWS
    vmem = lambda shape, kind=F32: pltpu.VMEM(shape, kind)
    scratch = [
        vmem((blocks, width)), vmem((blocks, width)), vmem((blocks, width), jnp.int32),
        vmem(destination.shape, jnp.int32), vmem(propagator.shape), vmem(transmit.shape), vmem(radiation.shape[1:]),
        vmem((2 * grid, grid)),
        vmem((2 * grid, 2 * grid), BF16), vmem((2 * grid, 2 * grid), BF16),
        vmem((2 * n_cuts, 6 * n_cuts), BF16), vmem((2 * n_cuts, 6 * n_cuts), BF16),
        vmem((2 * n_group, 6 * n_group), BF16),
        vmem((3 * blocks + 8, width)), vmem((3 * blocks + 8, width)),
        vmem((n_cuts * 8, width)),
        vmem((many, width)), vmem((many, width)),
        vmem((2 * many, width)), vmem((2 * many, width)),
        vmem(marks, BF16), vmem(marks, BF16),
        vmem((many, width), jnp.int32), vmem((many, width), jnp.int32),
        vmem((2, many, width)), vmem((2, many, width)),
        vmem((grid, 2 * grid)),
        vmem((2, n_active * 8, grid)), vmem((2, n_cuts * 8, grid)),
        vmem((2, n_cuts * 8, grid)), vmem((n_group * 8, grid)),
        vmem((n_group * 8, grid)), vmem((2, n_cuts * 8, grid)),
        vmem((2, n_cuts * 8, grid)), vmem((2, n_active * 8, grid)),
        vmem((n_cuts * 8, width)), vmem((n_cuts * 8, width)),
        pltpu.SemaphoreType.DMA((8,)), pltpu.SemaphoreType.DMA((13,)), pltpu.SemaphoreType.DMA((13,)),
    ]
    return pl.pallas_call(
        functools.partial(kernel, n_cuts, n_group, grid, blocks, width),
        out_shape=jax.ShapeDtypeStruct(radiation.shape, F32),
        in_specs=[pl.BlockSpec(memory_space=pl.ANY)] * 7,
        out_specs=pl.BlockSpec(memory_space=pl.ANY),
        scratch_shapes=scratch,
        compiler_params=pltpu.CompilerParams(collective_id=0, has_side_effects=True),
    )(radiation, phases, energy, pixels, destination, propagator, transmit)


def solution(mesh):
    sizes = dict(mesh.shape)
    return jax.shard_map(
        functools.partial(on_device, sizes["cuts"], sizes["group"]),
        mesh=mesh,
        in_specs=(
            P(("cuts", "group"), None, None, None),
            P(("cuts", "group"), None, None),
            P(("cuts", "group"), None, None),
            P(("cuts", "group"), None, None),
            P(("cuts", "group"), None),
            P(),
            P(),
        ),
        out_specs=P(("cuts", "group"), None, None, None),
        check_vma=False,
    )
```

```python
import contextlib
import functools
import math

import jax
import jax.numpy as jnp
from jax import lax
from jax.experimental import pallas as pl
from jax.experimental.pallas import tpu as pltpu
from jax.sharding import PartitionSpec as P

KICK_RATE = 0.5
PHASE_RATE = 1.0
EMIT_RATE = 0.5
F32 = jnp.float32
BF16 = jnp.bfloat16
MESH = pl.DeviceIdType.MESH
ROWS = 8
HALF = 4


def tag(name):
    return contextlib.nullcontext()


def iota(shape, dim):
    return lax.broadcasted_iota(jnp.int32, shape, dim)


def split(x):
    high = x.astype(BF16)
    return high, (x - high.astype(F32)).astype(BF16)


def dot(a, b):
    return jnp.dot(a, b, preferred_element_type=F32)


def dot_nt(a, b):
    return lax.dot_general(a, b, (((1,), (1,)), ((), ())), preferred_element_type=F32)


def dot_exact(a, b):
    return jnp.dot(a, b, precision=lax.Precision.HIGHEST, preferred_element_type=F32)


def turns(product, total):
    whole = jnp.floor((product + 0.5) * (1.0 / total))
    angle = (product - whole * total) * (2.0 * math.pi / total)
    return jnp.cos(angle), jnp.sin(angle)


def stack2(a, b, c, d):
    return jnp.concatenate(
        [jnp.concatenate([a, b], axis=1), jnp.concatenate([c, d], axis=1)], axis=0
    )


def triple(matrix):
    high, low = split(matrix)
    return jnp.concatenate([high, high, low], axis=1)


def apply_triple(packed, data):
    high, low = split(data)
    return dot(packed, jnp.concatenate([high, low, high], axis=0))


def kernel(
    n_cuts, n_group, grid, blocks, width,
    radiation, phases, energy, pixels, destination, propagator, transmit,
    out,
    phase_in, power_in, pixel_in, target_in, prop_in, gain_in, result_out,
    field, prop_hi, prop_lo, cut_fwd, cut_inv, mid_op,
    slip_a, got_a, slip_p, got_p, slip_b, got_b,
    hot_now, hot_next, turned_now, turned_next, row_now, row_next, read, weight, source,
    send1, recv1, send2, recv2, send3, recv3, send4, recv4, send_e, recv_e,
    load_sems, send_sems, recv_sems,
):
    c = lax.axis_index("cuts")
    g = lax.axis_index("group")
    total = n_cuts * n_group
    me = c * n_group + g
    n_active = grid // ROWS
    third = c // 3
    lane = c - 3 * third
    active = lane != 1
    idle = jnp.logical_not(active)
    side = lane // 2
    idle_cut = c - lane + 1
    half_group = n_group // 2
    my_active = 2 * third + side
    owner = jnp.where(active, c, c - 1 + 2 * (g // half_group))
    unit = jnp.where(active, g, n_group + g % half_group)
    many = 2 * n_cuts

    def wrap(value, size):
        return jnp.where(value >= size, value - size, value)

    def device(offset):
        other = wrap(me + (offset + total if offset < 0 else offset), total)
        return other // n_group, other % n_group

    def repeat(count, body):
        def step(i, carry):
            body(i)
            return carry
        lax.fori_loop(0, count, step, 0, unroll=math.gcd(count, 4))

    loads = [
        pltpu.make_async_copy(src, dst, load_sems.at[i])
        for i, (src, dst) in enumerate([
            (pixels.at[0], pixel_in), (radiation.at[0, 0], field.at[pl.ds(0, grid)]),
            (radiation.at[0, 1], field.at[pl.ds(grid, grid)]), (phases.at[0], phase_in),
            (energy.at[0], power_in), (destination, target_in), (propagator, prop_in), (transmit, gain_in),
        ])
    ]
    for load in loads:
        load.start()
    barrier = pltpu.get_barrier_semaphore()

    def hello(cc, gg):
        pl.semaphore_signal(barrier, inc=1, device_id=(cc, gg), device_id_type=MESH)

    ahead_group = wrap(g + 3, n_group)
    behind_group = wrap(g + n_group - 3, n_group)
    ring = max(1, n_cuts // 2)
    for j in sorted(range(n_cuts), key=lambda j: -min(j % ring, ring - j % ring)):
        cut = wrap(c + j, n_cuts)
        hello(cut, ahead_group)
        hello(cut, behind_group)
        if j:
            hello(cut, g)
    hello(*device(-1))
    hello(*device(1))

    @pl.when(active)
    def _():
        repeat(n_group - 1, lambda i: hello(c, wrap(g + 1 + i, n_group)))
        repeat(half_group, lambda i: hello(idle_cut, half_group * side + i))

    @pl.when(idle)
    def _():
        repeat(n_group, lambda i: hello(owner, wrap(g + i, n_group)))

    def meet():
        greeted = 2 + n_cuts - 1 + 2 * n_cuts

        @pl.when(active)
        def _():
            pl.semaphore_wait(barrier, greeted + n_group - 1 + half_group)

        @pl.when(idle)
        def _():
            pl.semaphore_wait(barrier, greeted + n_group)

    def remote(stage, src, dst, cc, gg):
        return pltpu.make_async_remote_copy(
            src_ref=src, dst_ref=dst, send_sem=send_sems.at[stage], recv_sem=recv_sems.at[stage],
            device_id=(cc, gg), device_id_type=MESH,
        )

    def push(stage, src, dst, cc, gg):
        mine = jnp.logical_and(cc == c, gg == g)

        @pl.when(mine)
        def _():
            pltpu.make_async_copy(src, dst, recv_sems.at[stage]).start()

        @pl.when(jnp.logical_not(mine))
        def _():
            remote(stage, src, dst, cc, gg).start()

    def arrived(stage, ref):
        with tag("wait%d" % stage):
            remote(stage, ref, ref, c, g).wait_recv()

    def sent(stage, ref):
        remote(stage, ref, ref, c, g).wait_send()

    def tile(ref, index):
        return ref.at[pl.ds(pl.multiple_of(index * 8, 8), 8)]

    shift = grid.bit_length()
    pairs = grid // 2
    places = 2 * grid

    def mark(count, cells, hot, rows, turned=None):
        rows[:count] = lax.shift_right_arithmetic(cells, shift)
        place = cells & (places - 1)
        for b in range(count):
            match = iota((places, width), 0) == jnp.broadcast_to(place[b:b + 1], (places, width))
            hot[:, b * width:(b + 1) * width] = jnp.where(match, 1.0, 0.0).astype(BF16)
        if turned is not None:
            columns = jnp.transpose(place.astype(F32))
            spot = iota((width, places), 1).astype(F32)
            for b in range(count):
                match = spot == jnp.broadcast_to(columns[:, b:b + 1], (width, places))
                turned[b * width:(b + 1) * width] = jnp.where(match, 1.0, 0.0).astype(BF16)

    def look(count, hot, rows):
        low = jnp.concatenate([field[pl.ds(0, grid, stride=2), :], field[pl.ds(1, grid, stride=2), :]], axis=1).astype(BF16)
        real, imag = [], []
        for two in range(count // 2):
            picked = dot(low, hot[:, two * 2 * width:(two + 1) * 2 * width])
            for b in range(2):
                at = rows[2 * two + b:2 * two + b + 1]
                match = iota((pairs, width), 0) == jnp.broadcast_to(at, (pairs, width))
                part = picked[:, b * width:(b + 1) * width]
                real.append(jnp.sum(jnp.where(match, part[:pairs], 0.0), axis=0, keepdims=True))
                imag.append(jnp.sum(jnp.where(match, part[pairs:], 0.0), axis=0, keepdims=True))
        read[0, :count] = jnp.concatenate(real, axis=0)
        read[1, :count] = jnp.concatenate(imag, axis=0)

    def kick(count, phase, power, cos, sin):
        power = power - KICK_RATE * (read[0, :count] * cos - read[1, :count] * sin)
        phase = phase + PHASE_RATE * power
        weight[0, :count] = jnp.cos(phase)
        weight[1, :count] = -jnp.sin(phase)
        return phase, power

    def deposit(count, hot, rows, turned=None):
        chunk = 8 if count % 8 == 0 else count
        shape = (pairs, width)
        gathered = jnp.zeros((grid, places), F32)
        for first in range(0, count, chunk):
            tops, bottoms = [], []
            for b in range(first, first + chunk):
                match = iota(shape, 0) == jnp.broadcast_to(rows[b:b + 1], shape)
                tops.append(jnp.where(match, jnp.broadcast_to(weight[0, b:b + 1], shape), 0.0).astype(BF16))
                bottoms.append(jnp.where(match, jnp.broadcast_to(weight[1, b:b + 1], shape), 0.0).astype(BF16))
            spread = jnp.concatenate([jnp.concatenate(tops, axis=1), jnp.concatenate(bottoms, axis=1)], axis=0)
            span = slice(first * width, (first + chunk) * width)
            if turned is None:
                gathered = gathered + dot_nt(spread, hot[:, span])
            else:
                gathered = gathered + dot(spread, turned[span])
        source[...] = gathered

    def emit():
        field[pl.ds(0, grid, stride=2), :] = field[pl.ds(0, grid, stride=2), :] + EMIT_RATE * source[:, :grid]
        field[pl.ds(1, grid, stride=2), :] = field[pl.ds(1, grid, stride=2), :] + EMIT_RATE * source[:, grid:]

    def diffract(keep):
        emit()
        high, low = split(field[...])
        both = dot(prop_hi[...], jnp.concatenate([high, low], axis=1))
        left = both[:, :grid] + both[:, grid:] + dot(prop_lo[...], high)
        left = jnp.concatenate([left[:grid], left[grid:]], axis=1)
        high, low = split(left)
        result = dot_nt(high, prop_hi[...]) + dot_nt(low, prop_hi[...]) + dot_nt(high, prop_lo[...])
        return jnp.where(keep, result, 0.0)

    def set_field(result):
        field[:grid] = result[:, :grid]
        field[grid:] = result[:, grid:]

    loads[0].wait()
    mark(blocks, pixel_in[...], hot_now, row_now)
    for load in loads[1:]:
        load.wait()
    look(blocks, hot_now, row_now)
    phase = phase_in[...]
    phase, power = kick(blocks, phase, power_in[...], jnp.cos(phase), jnp.sin(phase))
    slip_a[:blocks] = phase
    slip_a[blocks:2 * blocks] = power
    slip_a[2 * blocks:3 * blocks] = pixel_in[...].astype(F32)
    slip_a[3 * blocks:] = jnp.zeros_like(slip_a[3 * blocks:])
    slip_a[3 * blocks:3 * blocks + 1, :blocks] = target_in[...].astype(F32)
    with tag("meet"):
        meet()
    remote(0, slip_a, got_a, *device(-1)).start()
    prop = stack2(prop_in[0], -prop_in[1], prop_in[1], prop_in[0])
    high, low = split(prop)
    prop_hi[...] = high
    prop_lo[...] = low
    deposit(blocks, hot_now, row_now)
    set_field(diffract(me != total - 1))

    arrived(0, got_a)
    mark(blocks, got_a[2 * blocks:3 * blocks].astype(jnp.int32), hot_now, row_now)
    look(blocks, hot_now, row_now)
    phase = got_a[:blocks]
    phase, power = kick(blocks, phase, got_a[blocks:2 * blocks], jnp.cos(phase), jnp.sin(phase))
    deposit(blocks, hot_now, row_now)
    result = diffract(me != total - 2)
    for a in range(n_active):
        for h in range(2):
            at = a * ROWS + h * HALF
            send1[h, a * 8:a * 8 + HALF] = result[at:at + HALF, :grid]
            send1[h, a * 8 + HALF:(a + 1) * 8] = result[at:at + HALF, grid:]

    for h in range(2):
        def to_active(i):
            a = wrap(i + my_active, n_active)
            push(1 + h, tile(send1.at[h], a), tile(recv1.at[h], c), 3 * (a >> 1) + 2 * (a & 1), g)
        repeat(n_active, to_active)

    target = got_a[3 * blocks:3 * blocks + 1, :blocks]
    square = (blocks, blocks)
    wide = jnp.broadcast_to(target, square)
    tall = jnp.sum(jnp.where(iota(square, 0) == iota(square, 1), wide, 0.0), axis=1, keepdims=True)
    same = jnp.logical_and(jnp.broadcast_to(tall, square) == wide, iota(square, 0) < iota(square, 1))
    rank = jnp.sum(jnp.where(same, 1.0, 0.0), axis=0, keepdims=True)
    payload = jnp.concatenate([phase, power, got_a[2 * blocks:3 * blocks] + 1.0], axis=1)
    shape = (n_cuts, blocks)
    goes = jnp.broadcast_to(target, shape) == iota(shape, 0).astype(F32)
    send_e[...] = jnp.zeros_like(send_e)
    for slot in range(2):
        pick = jnp.logical_and(goes, jnp.broadcast_to(rank, shape) == float(slot))
        moved = dot_exact(jnp.where(pick, 1.0, 0.0), payload)
        for part in range(3):
            send_e[pl.ds(slot * 3 + part, n_cuts, stride=8), :] = moved[:, part * width:(part + 1) * width]
    carry_cut = jnp.where(jnp.logical_and(g >= n_group - 3, g <= n_group - 2), 1, 0)

    def to_cut(i):
        k = wrap(i + c, n_cuts)
        remote(9, tile(send_e, k), tile(recv_e, c), wrap(k + carry_cut, n_cuts), ahead_group).start()

    shape = (n_cuts, n_cuts)
    g_real = g.astype(F32)
    cos, sin = turns((iota(shape, 1).astype(F32) * n_group + g_real) * iota(shape, 0).astype(F32), total)
    cut_fwd[...] = triple(stack2(cos, sin, -sin, cos))
    cos, sin = turns((iota(shape, 0).astype(F32) * n_group + g_real) * iota(shape, 1).astype(F32), total)
    cut_inv[...] = triple(stack2(cos, -sin, sin, cos))
    first_freq = unit // 2
    shape = (n_group, total)
    chosen = iota(shape, 1) == first_freq + n_cuts * iota(shape, 0)
    gain_real = jnp.sum(jnp.where(chosen, jnp.broadcast_to(gain_in[0:1], shape), 0.0), axis=1, keepdims=True)
    gain_imag = jnp.sum(jnp.where(chosen, jnp.broadcast_to(gain_in[1:2], shape), 0.0), axis=1, keepdims=True)
    shape = (n_group, n_group)
    lag_cos, lag_sin = turns((first_freq.astype(F32) + n_cuts * iota(shape, 0).astype(F32)) * 4.0, total)
    scale = 1.0 / total
    turn_real = (gain_real * lag_cos + gain_imag * lag_sin) * scale
    turn_imag = (gain_imag * lag_cos - gain_real * lag_sin) * scale
    cos, sin = turns(iota(shape, 0).astype(F32) * iota(shape, 1).astype(F32), n_group)
    shaped_real = turn_real * cos + turn_imag * sin
    shaped_imag = turn_imag * cos - turn_real * sin
    mid_op[...] = triple(dot_exact(
        stack2(cos, -sin, sin, cos), stack2(shaped_real, -shaped_imag, shaped_imag, shaped_real)
    ))

    def apply(operator, count, source_ref, target_ref):
        real = [source_ref[pl.ds(j, count, stride=8), :] for j in range(HALF)]
        imag = [source_ref[pl.ds(HALF + j, count, stride=8), :] for j in range(HALF)]
        data = jnp.concatenate([jnp.concatenate(real, axis=1), jnp.concatenate(imag, axis=1)], axis=0)
        done = apply_triple(operator[...], data)
        for j in range(HALF):
            target_ref[pl.ds(j, count, stride=8), :] = done[:count, j * grid:(j + 1) * grid]
            target_ref[pl.ds(HALF + j, count, stride=8), :] = done[count:, j * grid:(j + 1) * grid]

    @pl.when(active)
    def _():
        for h in range(2):
            arrived(1 + h, recv1.at[h])
            with tag("fwd%d" % h):
                apply(cut_fwd, n_cuts, recv1.at[h], send2.at[h])
            def to_unit(i):
                freq = wrap(i + (3 * g) // 4, n_cuts)
                u = 2 * freq + h
                own = u < n_group
                push(
                    3, tile(send2.at[h], freq), tile(recv2, g),
                    jnp.where(own, c, idle_cut), jnp.where(own, u, half_group * side + u - n_group),
                )
            with tag("send2%d" % h):
                repeat(n_cuts, to_unit)
        with tag("sende"):
            repeat(n_cuts, to_cut)

    arrived(3, recv2)
    with tag("mid"):
        apply(mid_op, n_group, recv2, send3)

    for h in range(2):
        @pl.when((unit & 1) == h)
        def _():
            def to_owner(i):
                m = wrap(i + g, n_group)
                push(4 + h, tile(send3, m), tile(recv3.at[h], unit >> 1), owner, m)
            with tag("send3"):
                repeat(n_group, to_owner)

    @pl.when(idle)
    def _():
        with tag("sende"):
            repeat(n_cuts, to_cut)

    @pl.when(active)
    def _():
        for h in range(2):
            arrived(4 + h, recv3.at[h])
            with tag("inv%d" % h):
                apply(cut_inv, n_cuts, recv3.at[h], send4.at[h])
            def to_slice(i):
                k = wrap(i + c, n_cuts)
                push(6 + h, tile(send4.at[h], k), tile(recv4.at[h], my_active), k, g)
            with tag("send4%d" % h):
                repeat(n_cuts, to_slice)

    arrived(9, recv_e)

    def pieces(part):
        return jnp.concatenate(
            [recv_e[pl.ds(part, n_cuts, stride=8), :], recv_e[pl.ds(3 + part, n_cuts, stride=8), :]], axis=0
        )

    def cells_of(value):
        return (value + 0.25).astype(jnp.int32) - 1

    cells = pieces(2)
    slip_p[...] = cells
    remote(11, slip_p, got_p, *device(-1)).start()
    with tag("mark3"):
        mark(many, cells_of(cells), hot_now, row_now, turned_now)
    phase = pieces(0)
    cos, sin = jnp.cos(phase), jnp.sin(phase)
    arrived(11, got_p)
    with tag("mark4"):
        mark(many, cells_of(got_p[...]), hot_next, row_next, turned_next)
    for h in range(2):
        arrived(6 + h, recv4.at[h])
        for a in range(n_active):
            at = a * ROWS + h * HALF
            field[at:at + HALF] = recv4[h, a * 8:a * 8 + HALF]
            field[grid + at:grid + at + HALF] = recv4[h, a * 8 + HALF:(a + 1) * 8]

    with tag("look3"):
        look(many, hot_now, row_now)
    with tag("kick3"):
        phase, power = kick(many, phase, pieces(1), cos, sin)
        slip_b[:many] = phase
        slip_b[many:] = power
    remote(12, slip_b, got_b, *device(-1)).start()
    with tag("deposit3"):
        deposit(many, hot_now, row_now, turned_now)
    with tag("diffract3"):
        set_field(diffract(me != 1))

    with tag("look4"):
        look(many, hot_next, row_next)
    arrived(12, got_b)
    with tag("kick4"):
        phase = got_b[:many]
        kick(many, phase, got_b[many:], jnp.cos(phase), jnp.sin(phase))
    with tag("deposit4"):
        deposit(many, hot_next, row_next, turned_next)
    with tag("diffract4"):
        result = diffract(me != 0)
        result_out[0] = result[:, :grid]
        result_out[1] = result[:, grid:]
    store = pltpu.make_async_copy(result_out, out.at[0], load_sems.at[0])
    store.start()

    sent(0, slip_a)
    sent(9, send_e)
    sent(11, slip_p)
    sent(12, slip_b)

    @pl.when(active)
    def _():
        for h in range(2):
            sent(1 + h, send1.at[h, pl.ds(0, (n_active - 1) * 8)])
            sent(6 + h, send4.at[h, pl.ds(0, (n_cuts - 1) * 8)])
        for h in range(2):
            @pl.when((unit & 1) == h)
            def _():
                sent(4 + h, send3.at[pl.ds(0, (n_group - 1) * 8)])
        sent(3, send2.at[0])
        sent(3, send2.at[1, pl.ds(0, (n_cuts - 1) * 8)])

    @pl.when(idle)
    def _():
        for h in range(2):
            sent(1 + h, send1.at[h])
            @pl.when((unit & 1) == h)
            def _():
                sent(4 + h, send3)
    store.wait()


def on_device(n_cuts, n_group, radiation, phases, energy, pixels, destination, propagator, transmit):
    grid = radiation.shape[-1]
    blocks, width = phases.shape[1:]
    many = 2 * n_cuts
    n_active = grid // ROWS
    vmem = lambda shape, kind=F32: pltpu.VMEM(shape, kind)
    scratch = [
        vmem((blocks, width)), vmem((blocks, width)), vmem((blocks, width), jnp.int32),
        vmem(destination.shape, jnp.int32), vmem(propagator.shape), vmem(transmit.shape), vmem(radiation.shape[1:]),
        vmem((2 * grid, grid)),
        vmem((2 * grid, 2 * grid), BF16), vmem((2 * grid, 2 * grid), BF16),
        vmem((2 * n_cuts, 6 * n_cuts), BF16), vmem((2 * n_cuts, 6 * n_cuts), BF16),
        vmem((2 * n_group, 6 * n_group), BF16),
        vmem((3 * blocks + 8, width)), vmem((3 * blocks + 8, width)),
        vmem((many, width)), vmem((many, width)),
        vmem((2 * many, width)), vmem((2 * many, width)),
        vmem((2 * grid, many * width), BF16), vmem((2 * grid, many * width), BF16),
        vmem((many * width, 2 * grid), BF16), vmem((many * width, 2 * grid), BF16),
        vmem((many, width), jnp.int32), vmem((many, width), jnp.int32),
        vmem((2, many, width)), vmem((2, many, width)),
        vmem((grid, 2 * grid)),
        vmem((2, n_active * 8, grid)), vmem((2, n_cuts * 8, grid)),
        vmem((2, n_cuts * 8, grid)), vmem((n_group * 8, grid)),
        vmem((n_group * 8, grid)), vmem((2, n_cuts * 8, grid)),
        vmem((2, n_cuts * 8, grid)), vmem((2, n_active * 8, grid)),
        vmem((n_cuts * 8, width)), vmem((n_cuts * 8, width)),
        pltpu.SemaphoreType.DMA((8,)), pltpu.SemaphoreType.DMA((13,)), pltpu.SemaphoreType.DMA((13,)),
    ]
    return pl.pallas_call(
        functools.partial(kernel, n_cuts, n_group, grid, blocks, width),
        out_shape=jax.ShapeDtypeStruct(radiation.shape, F32),
        in_specs=[pl.BlockSpec(memory_space=pltpu.HBM)] * 7,
        out_specs=pl.BlockSpec(memory_space=pl.ANY),
        scratch_shapes=scratch,
        compiler_params=pltpu.CompilerParams(collective_id=0, has_side_effects=True, vmem_limit_bytes=32 << 20),
    )(*(
        pltpu.with_memory_space_constraint(x, pltpu.HBM)
        for x in (radiation, phases, energy, pixels, destination, propagator, transmit)
    ))


def solution(mesh):
    sizes = dict(mesh.shape)
    return jax.shard_map(
        functools.partial(on_device, sizes["cuts"], sizes["group"]),
        mesh=mesh,
        in_specs=(
            P(("cuts", "group"), None, None, None),
            P(("cuts", "group"), None, None),
            P(("cuts", "group"), None, None),
            P(("cuts", "group"), None, None),
            P(("cuts", "group"), None),
            P(),
            P(),
        ),
        out_specs=P(("cuts", "group"), None, None, None),
        check_vma=False,
    )
```

```python
import contextlib
import functools
import math

import jax
import jax.numpy as jnp
from jax import lax
from jax.experimental import pallas as pl
from jax.experimental.pallas import tpu as pltpu
from jax.sharding import PartitionSpec as P

KICK_RATE = 0.5
PHASE_RATE = 1.0
EMIT_RATE = 0.5
F32 = jnp.float32
BF16 = jnp.bfloat16
MESH = pl.DeviceIdType.MESH
ROWS = 8
HALF = 4


def tag(name):
    return contextlib.nullcontext()


def iota(shape, dim):
    return lax.broadcasted_iota(jnp.int32, shape, dim)


def split(x):
    high = x.astype(BF16)
    return high, (x - high.astype(F32)).astype(BF16)


def dot(a, b):
    return jnp.dot(a, b, preferred_element_type=F32)


def dot_nt(a, b):
    return lax.dot_general(a, b, (((1,), (1,)), ((), ())), preferred_element_type=F32)


def dot_exact(a, b):
    return jnp.dot(a, b, precision=lax.Precision.HIGHEST, preferred_element_type=F32)


def turns(product, total):
    whole = jnp.floor((product + 0.5) * (1.0 / total))
    angle = (product - whole * total) * (2.0 * math.pi / total)
    return jnp.cos(angle), jnp.sin(angle)


def stack2(a, b, c, d):
    return jnp.concatenate(
        [jnp.concatenate([a, b], axis=1), jnp.concatenate([c, d], axis=1)], axis=0
    )


def triple(matrix):
    high, low = split(matrix)
    return jnp.concatenate([high, high, low], axis=1)


def apply_triple(packed, data):
    high, low = split(data)
    return dot(packed, jnp.concatenate([high, low, high], axis=0))


def kernel(
    n_cuts, n_group, grid, blocks, width,
    radiation, phases, energy, pixels, destination, propagator, transmit,
    out,
    phase_in, power_in, pixel_in, target_in, prop_in, gain_in, result_out,
    field, prop_hi, prop_lo, cut_fwd, cut_inv, mid_op,
    slip_a, got_a, slip_p, got_p, slip_b, got_b,
    hot_now, hot_next, turned_now, turned_next, row_now, row_next, read, weight, source,
    send1, recv1, send2, recv2, send3, recv3, send4, recv4, send_e, recv_e,
    go_sem, load_sems, send_sems, recv_sems,
):
    c = lax.axis_index("cuts")
    g = lax.axis_index("group")
    total = n_cuts * n_group
    me = c * n_group + g
    n_active = grid // ROWS
    third = c // 3
    lane = c - 3 * third
    active = lane != 1
    idle = jnp.logical_not(active)
    side = lane // 2
    idle_cut = c - lane + 1
    half_group = n_group // 2
    my_active = 2 * third + side
    owner = jnp.where(active, c, c - 1 + 2 * (g // half_group))
    unit = jnp.where(active, g, n_group + g % half_group)
    many = 2 * n_cuts

    def wrap(value, size):
        return jnp.where(value >= size, value - size, value)

    def device(offset):
        other = wrap(me + (offset + total if offset < 0 else offset), total)
        return other // n_group, other % n_group

    def repeat(count, body):
        def step(i, carry):
            body(i)
            return carry
        lax.fori_loop(0, count, step, 0, unroll=math.gcd(count, 4))

    loads = [
        pltpu.make_async_copy(src, dst, load_sems.at[i])
        for i, (src, dst) in enumerate([
            (pixels.at[0], pixel_in), (radiation.at[0, 0], field.at[pl.ds(0, grid)]),
            (radiation.at[0, 1], field.at[pl.ds(grid, grid)]), (phases.at[0], phase_in),
            (energy.at[0], power_in), (destination, target_in), (propagator, prop_in), (transmit, gain_in),
        ])
    ]
    for load in loads:
        load.start()
    barrier = pltpu.get_barrier_semaphore()

    def hello(cc, gg):
        pl.semaphore_signal(barrier, inc=1, device_id=(cc, gg), device_id_type=MESH)

    ahead_group = wrap(g + 3, n_group)
    behind_group = wrap(g + n_group - 3, n_group)
    ring = n_cuts // 2
    cut_order = sorted(range(n_cuts), key=lambda j: -min(j % ring, ring - j % ring))
    quads = n_group // 4
    quad_order = sorted(range(quads), key=lambda j: -min(j, quads - j))
    quad = g // 4
    for j in cut_order:
        cut = wrap(c + j, n_cuts)
        hello(cut, ahead_group)
        hello(cut, behind_group)
        if j:
            hello(cut, g)
    hello(*device(-1))
    hello(*device(1))

    @pl.when(active)
    def _():
        repeat(n_group - 1, lambda i: hello(c, wrap(g + 1 + i, n_group)))
        repeat(half_group, lambda i: hello(idle_cut, half_group * side + i))

    @pl.when(idle)
    def _():
        repeat(n_group, lambda i: hello(owner, wrap(g + i, n_group)))

    def meet():
        greeted = 2 + n_cuts - 1 + 2 * n_cuts

        @pl.when(active)
        def _():
            pl.semaphore_wait(barrier, greeted + n_group - 1 + half_group)

        @pl.when(idle)
        def _():
            pl.semaphore_wait(barrier, greeted + n_group)

    def remote(stage, src, dst, cc, gg):
        return pltpu.make_async_remote_copy(
            src_ref=src, dst_ref=dst, send_sem=send_sems.at[stage], recv_sem=recv_sems.at[stage],
            device_id=(cc, gg), device_id_type=MESH,
        )

    def keep(stage, src, dst):
        pltpu.make_async_copy(src, dst, recv_sems.at[stage]).start()

    def push(mine, stage, src, dst, cc, gg):
        @pl.when(mine)
        def _():
            keep(stage, src, dst)

        @pl.when(jnp.logical_not(mine))
        def _():
            remote(stage, src, dst, cc, gg).start()

    def arrived(stage, ref):
        with tag("wait%d" % stage):
            remote(stage, ref, ref, c, g).wait_recv()

    def sent(stage, ref):
        remote(stage, ref, ref, c, g).wait_send()

    def tile(ref, index):
        return ref.at[pl.ds(pl.multiple_of(index * 8, 8), 8)]

    shift = grid.bit_length()
    pairs = grid // 2
    places = 2 * grid

    def low_rows(value, size):
        packed = jnp.broadcast_to(value, (16, width)).astype(BF16)
        return jnp.broadcast_to(packed[None], (size // 16, 16, width)).reshape(size, width)

    def mark(count, cells, hot, rows, turned):
        rows[:count] = lax.shift_right_arithmetic(cells, shift)
        place = (cells & (places - 1)).astype(F32)
        spots = iota((places, width), 0).astype(F32).astype(BF16)
        one, zero = jnp.ones((places, width), BF16), jnp.zeros((places, width), BF16)
        for b in range(count):
            hot[:, b * width:(b + 1) * width] = jnp.where(spots == low_rows(place[b:b + 1], places), one, zero)
        columns = jnp.transpose(place)
        spots = iota((width, grid), 1).astype(F32).astype(BF16)
        one, zero = jnp.ones((width, grid), BF16), jnp.zeros((width, grid), BF16)
        for b in range(count):
            column = jnp.broadcast_to(columns[:, b:b + 1], (width, grid))
            for q in range(2):
                match = spots == (column - float(q * grid)).astype(BF16)
                turned[b * width:(b + 1) * width, q * grid:(q + 1) * grid] = jnp.where(match, one, zero)

    def look(count, hot, rows):
        low = jnp.concatenate([field[pl.ds(0, grid, stride=2), :], field[pl.ds(1, grid, stride=2), :]], axis=1).astype(BF16)
        real, imag = [], []
        for two in range(count // 2):
            picked = dot(low, hot[:, two * 2 * width:(two + 1) * 2 * width])
            for b in range(2):
                at = rows[2 * two + b:2 * two + b + 1]
                match = iota((pairs, width), 0) == jnp.broadcast_to(at, (pairs, width))
                part = picked[:, b * width:(b + 1) * width]
                real.append(jnp.sum(jnp.where(match, part[:pairs], 0.0), axis=0, keepdims=True))
                imag.append(jnp.sum(jnp.where(match, part[pairs:], 0.0), axis=0, keepdims=True))
        read[0, :count] = jnp.concatenate(real, axis=0)
        read[1, :count] = jnp.concatenate(imag, axis=0)

    def kick(count, phase, power, cos, sin):
        power = power - KICK_RATE * (read[0, :count] * cos - read[1, :count] * sin)
        phase = phase + PHASE_RATE * power
        weight[0, :count] = jnp.cos(phase)
        weight[1, :count] = -jnp.sin(phase)
        return phase, power

    def deposit(count, rows, turned):
        chunk = 8 if count % 8 == 0 else count
        gathered = jnp.zeros((grid, places), F32)
        spots = iota((pairs, width), 0).astype(F32).astype(BF16)
        zero = jnp.zeros((pairs, width), BF16)
        for first in range(0, count, chunk):
            tops, bottoms = [], []
            for b in range(first, first + chunk):
                match = spots == low_rows(rows[b:b + 1].astype(F32), pairs)
                tops.append(jnp.where(match, low_rows(weight[0, b:b + 1], pairs), zero))
                bottoms.append(jnp.where(match, low_rows(weight[1, b:b + 1], pairs), zero))
            spread = jnp.concatenate([jnp.concatenate(tops, axis=1), jnp.concatenate(bottoms, axis=1)], axis=0)
            gathered = gathered + dot(spread, turned[first * width:(first + chunk) * width])
        source[...] = gathered

    def emit():
        field[pl.ds(0, grid, stride=2), :] = field[pl.ds(0, grid, stride=2), :] + EMIT_RATE * source[:, :grid]
        field[pl.ds(1, grid, stride=2), :] = field[pl.ds(1, grid, stride=2), :] + EMIT_RATE * source[:, grid:]

    def diffract(keep):
        emit()
        high, low = split(field[...])
        both = dot(prop_hi[...], jnp.concatenate([high, low], axis=1))
        left = both[:, :grid] + both[:, grid:] + dot(prop_lo[...], high)
        left = jnp.concatenate([left[:grid], left[grid:]], axis=1)
        high, low = split(left)
        result = dot_nt(high, prop_hi[...]) + dot_nt(low, prop_hi[...]) + dot_nt(high, prop_lo[...])
        return jnp.where(keep, result, 0.0)

    def set_field(result):
        field[:grid] = result[:, :grid]
        field[grid:] = result[:, grid:]

    loads[0].wait()
    mark(blocks, pixel_in[...], hot_now, row_now, turned_now)
    for load in loads[1:]:
        load.wait()
    look(blocks, hot_now, row_now)
    phase = phase_in[...]
    phase, power = kick(blocks, phase, power_in[...], jnp.cos(phase), jnp.sin(phase))
    slip_a[:blocks] = phase
    slip_a[blocks:2 * blocks] = power
    slip_a[2 * blocks:3 * blocks] = pixel_in[...].astype(F32)
    slip_a[3 * blocks:] = jnp.zeros_like(slip_a[3 * blocks:])
    slip_a[3 * blocks:3 * blocks + 1, :blocks] = target_in[...].astype(F32)
    with tag("meet"):
        meet()
    remote(0, slip_a, got_a, *device(-1)).start()
    prop = stack2(prop_in[0], -prop_in[1], prop_in[1], prop_in[0])
    high, low = split(prop)
    prop_hi[...] = high
    prop_lo[...] = low
    deposit(blocks, row_now, turned_now)
    set_field(diffract(me != total - 1))

    arrived(0, got_a)
    mark(blocks, got_a[2 * blocks:3 * blocks].astype(jnp.int32), hot_now, row_now, turned_now)
    look(blocks, hot_now, row_now)
    phase = got_a[:blocks]
    phase, power = kick(blocks, phase, got_a[blocks:2 * blocks], jnp.cos(phase), jnp.sin(phase))
    deposit(blocks, row_now, turned_now)
    result = diffract(me != total - 2)
    for a in range(n_active):
        for h in range(2):
            at = a * ROWS + h * HALF
            send1[h, a * 8:a * 8 + HALF] = result[at:at + HALF, :grid]
            send1[h, a * 8 + HALF:(a + 1) * 8] = result[at:at + HALF, grid:]

    for j in cut_order:
        cut = wrap(c + j, n_cuts)
        row = (cut * 43) >> 7
        place = cut - 3 * row

        @pl.when(place != 1)
        def _():
            a = 2 * row + (place >> 1)
            for h in range(2):
                if j:
                    remote(1 + h, tile(send1.at[h], a), tile(recv1.at[h], c), cut, g).start()
                else:
                    keep(1 + h, tile(send1.at[h], a), tile(recv1.at[h], c))

    target = got_a[3 * blocks:3 * blocks + 1, :blocks]
    square = (blocks, blocks)
    wide = jnp.broadcast_to(target, square)
    tall = jnp.sum(jnp.where(iota(square, 0) == iota(square, 1), wide, 0.0), axis=1, keepdims=True)
    same = jnp.logical_and(jnp.broadcast_to(tall, square) == wide, iota(square, 0) < iota(square, 1))
    rank = jnp.sum(jnp.where(same, 1.0, 0.0), axis=0, keepdims=True)
    payload = jnp.concatenate([phase, power, got_a[2 * blocks:3 * blocks] + 1.0], axis=1)
    shape = (n_cuts, blocks)
    goes = jnp.broadcast_to(target, shape) == iota(shape, 0).astype(F32)
    send_e[...] = jnp.zeros_like(send_e)
    for slot in range(2):
        pick = jnp.logical_and(goes, jnp.broadcast_to(rank, shape) == float(slot))
        moved = dot_exact(jnp.where(pick, 1.0, 0.0), payload)
        for part in range(3):
            send_e[pl.ds(slot * 3 + part, n_cuts, stride=8), :] = moved[:, part * width:(part + 1) * width]
    carry_cut = jnp.where(jnp.logical_and(g >= n_group - 3, g <= n_group - 2), 1, 0)

    def send_electrons():
        for j in cut_order:
            cut = wrap(c + j, n_cuts)
            k = wrap(cut + n_cuts - carry_cut, n_cuts)
            remote(9, tile(send_e, k), tile(recv_e, c), cut, ahead_group).start()

    shape = (n_cuts, n_cuts)
    g_real = g.astype(F32)
    cos, sin = turns((iota(shape, 1).astype(F32) * n_group + g_real) * iota(shape, 0).astype(F32), total)
    cut_fwd[...] = triple(stack2(cos, sin, -sin, cos))
    cos, sin = turns((iota(shape, 0).astype(F32) * n_group + g_real) * iota(shape, 1).astype(F32), total)
    cut_inv[...] = triple(stack2(cos, -sin, sin, cos))
    first_freq = unit // 2
    shape = (n_group, total)
    chosen = iota(shape, 1) == first_freq + n_cuts * iota(shape, 0)
    gain_real = jnp.sum(jnp.where(chosen, jnp.broadcast_to(gain_in[0:1], shape), 0.0), axis=1, keepdims=True)
    gain_imag = jnp.sum(jnp.where(chosen, jnp.broadcast_to(gain_in[1:2], shape), 0.0), axis=1, keepdims=True)
    shape = (n_group, n_group)
    lag_cos, lag_sin = turns((first_freq.astype(F32) + n_cuts * iota(shape, 0).astype(F32)) * 4.0, total)
    scale = 1.0 / total
    turn_real = (gain_real * lag_cos + gain_imag * lag_sin) * scale
    turn_imag = (gain_imag * lag_cos - gain_real * lag_sin) * scale
    cos, sin = turns(iota(shape, 0).astype(F32) * iota(shape, 1).astype(F32), n_group)
    shaped_real = turn_real * cos + turn_imag * sin
    shaped_imag = turn_imag * cos - turn_real * sin
    mid_op[...] = triple(dot_exact(
        stack2(cos, -sin, sin, cos), stack2(shaped_real, -shaped_imag, shaped_imag, shaped_real)
    ))

    def apply(operator, count, source_ref, target_ref):
        real = [source_ref[pl.ds(j, count, stride=8), :] for j in range(HALF)]
        imag = [source_ref[pl.ds(HALF + j, count, stride=8), :] for j in range(HALF)]
        data = jnp.concatenate([jnp.concatenate(real, axis=1), jnp.concatenate(imag, axis=1)], axis=0)
        done = apply_triple(operator[...], data)
        for j in range(HALF):
            target_ref[pl.ds(j, count, stride=8), :] = done[:count, j * grid:(j + 1) * grid]
            target_ref[pl.ds(HALF + j, count, stride=8), :] = done[count:, j * grid:(j + 1) * grid]

    @pl.when(active)
    def _():
        for h in range(2):
            arrived(1 + h, recv1.at[h])
            with tag("fwd%d" % h):
                apply(cut_fwd, n_cuts, recv1.at[h], send2.at[h])
        with tag("send2"):
            for j in quad_order:
                y = wrap(quad + j, quads)
                for r in range(4):
                    src, dst = tile(send2.at[r % 2], 2 * y + r // 2), tile(recv2, g)
                    if j:
                        remote(3, src, dst, c, 4 * y + r).start()
                    else:
                        push(4 * y + r == g, 3, src, dst, c, 4 * y + r)
                low = y - side * (quads // 2)

                @pl.when(jnp.logical_and(low >= 0, low < quads // 2))
                def _():
                    for r in range(4):
                        src = tile(send2.at[r % 2], n_group // 2 + 2 * low + r // 2)
                        remote(3, src, tile(recv2, g), idle_cut, 4 * y + r).start()

        @pl.when(side == g // half_group)
        def _():
            pl.semaphore_signal(go_sem, inc=1, device_id=(idle_cut, g), device_id_type=MESH)

        with tag("sende"):
            send_electrons()

    @pl.when(idle)
    def _():
        with tag("go"):
            pl.semaphore_wait(go_sem, 1)
        send_electrons()

    arrived(3, recv2)
    with tag("mid"):
        apply(mid_op, n_group, recv2, send3)

    for h in range(2):
        @pl.when((unit & 1) == h)
        def _():
            with tag("send3"):
                for j in quad_order:
                    y = wrap(quad + j, quads)
                    for r in range(4):
                        src, dst = tile(send3, 4 * y + r), tile(recv3.at[h], unit >> 1)
                        if j:
                            remote(4 + h, src, dst, owner, 4 * y + r).start()
                        else:
                            push(jnp.logical_and(active, 4 * y + r == g), 4 + h, src, dst, owner, 4 * y + r)

    @pl.when(active)
    def _():
        for h in range(2):
            arrived(4 + h, recv3.at[h])
            with tag("inv%d" % h):
                apply(cut_inv, n_cuts, recv3.at[h], send4.at[h])
        with tag("send4"):
            for j in cut_order:
                cut = wrap(c + j, n_cuts)
                for h in range(2):
                    src, dst = tile(send4.at[h], cut), tile(recv4.at[h], my_active)
                    if j:
                        remote(6 + h, src, dst, cut, g).start()
                    else:
                        keep(6 + h, src, dst)

    arrived(9, recv_e)

    def pieces(part):
        return jnp.concatenate(
            [recv_e[pl.ds(part, n_cuts, stride=8), :], recv_e[pl.ds(3 + part, n_cuts, stride=8), :]], axis=0
        )

    def cells_of(value):
        return (value + 0.25).astype(jnp.int32) - 1

    cells = pieces(2)
    slip_p[...] = cells
    remote(11, slip_p, got_p, *device(-1)).start()
    with tag("mark3"):
        mark(many, cells_of(cells), hot_now, row_now, turned_now)
    phase = pieces(0)
    cos, sin = jnp.cos(phase), jnp.sin(phase)
    arrived(11, got_p)
    with tag("mark4"):
        mark(many, cells_of(got_p[...]), hot_next, row_next, turned_next)
    for h in range(2):
        arrived(6 + h, recv4.at[h])
        for a in range(n_active):
            at = a * ROWS + h * HALF
            field[at:at + HALF] = recv4[h, a * 8:a * 8 + HALF]
            field[grid + at:grid + at + HALF] = recv4[h, a * 8 + HALF:(a + 1) * 8]

    with tag("look3"):
        look(many, hot_now, row_now)
    with tag("kick3"):
        phase, power = kick(many, phase, pieces(1), cos, sin)
        slip_b[:many] = phase
        slip_b[many:] = power
    remote(12, slip_b, got_b, *device(-1)).start()
    with tag("deposit3"):
        deposit(many, row_now, turned_now)
    with tag("diffract3"):
        set_field(diffract(me != 1))

    with tag("look4"):
        look(many, hot_next, row_next)
    arrived(12, got_b)
    with tag("kick4"):
        phase = got_b[:many]
        kick(many, phase, got_b[many:], jnp.cos(phase), jnp.sin(phase))
    with tag("deposit4"):
        deposit(many, row_next, turned_next)
    with tag("diffract4"):
        result = diffract(me != 0)
        result_out[0] = result[:, :grid]
        result_out[1] = result[:, grid:]
    store = pltpu.make_async_copy(result_out, out.at[0], load_sems.at[0])
    store.start()

    sent(0, slip_a)
    sent(9, send_e)
    sent(11, slip_p)
    sent(12, slip_b)

    @pl.when(active)
    def _():
        for h in range(2):
            sent(1 + h, send1.at[h, pl.ds(0, (n_active - 1) * 8)])
            sent(6 + h, send4.at[h, pl.ds(0, (n_cuts - 1) * 8)])
        for h in range(2):
            @pl.when((unit & 1) == h)
            def _():
                sent(4 + h, send3.at[pl.ds(0, (n_group - 1) * 8)])
        sent(3, send2.at[0])
        sent(3, send2.at[1, pl.ds(0, (n_cuts - 1) * 8)])

    @pl.when(idle)
    def _():
        for h in range(2):
            sent(1 + h, send1.at[h])
            @pl.when((unit & 1) == h)
            def _():
                sent(4 + h, send3)
    store.wait()


def on_device(n_cuts, n_group, radiation, phases, energy, pixels, destination, propagator, transmit):
    grid = radiation.shape[-1]
    blocks, width = phases.shape[1:]
    many = 2 * n_cuts
    n_active = grid // ROWS
    vmem = lambda shape, kind=F32: pltpu.VMEM(shape, kind)
    scratch = [
        vmem((blocks, width)), vmem((blocks, width)), vmem((blocks, width), jnp.int32),
        vmem(destination.shape, jnp.int32), vmem(propagator.shape), vmem(transmit.shape), vmem(radiation.shape[1:]),
        vmem((2 * grid, grid)),
        vmem((2 * grid, 2 * grid), BF16), vmem((2 * grid, 2 * grid), BF16),
        vmem((2 * n_cuts, 6 * n_cuts), BF16), vmem((2 * n_cuts, 6 * n_cuts), BF16),
        vmem((2 * n_group, 6 * n_group), BF16),
        vmem((3 * blocks + 8, width)), vmem((3 * blocks + 8, width)),
        vmem((many, width)), vmem((many, width)),
        vmem((2 * many, width)), vmem((2 * many, width)),
        vmem((2 * grid, many * width), BF16), vmem((2 * grid, many * width), BF16),
        vmem((many * width, 2 * grid), BF16), vmem((many * width, 2 * grid), BF16),
        vmem((many, width), jnp.int32), vmem((many, width), jnp.int32),
        vmem((2, many, width)), vmem((2, many, width)),
        vmem((grid, 2 * grid)),
        vmem((2, n_active * 8, grid)), vmem((2, n_cuts * 8, grid)),
        vmem((2, n_cuts * 8, grid)), vmem((n_group * 8, grid)),
        vmem((n_group * 8, grid)), vmem((2, n_cuts * 8, grid)),
        vmem((2, n_cuts * 8, grid)), vmem((2, n_active * 8, grid)),
        vmem((n_cuts * 8, width)), vmem((n_cuts * 8, width)),
        pltpu.SemaphoreType.REGULAR, pltpu.SemaphoreType.DMA((8,)), pltpu.SemaphoreType.DMA((13,)), pltpu.SemaphoreType.DMA((13,)),
    ]
    return pl.pallas_call(
        functools.partial(kernel, n_cuts, n_group, grid, blocks, width),
        out_shape=jax.ShapeDtypeStruct(radiation.shape, F32),
        in_specs=[pl.BlockSpec(memory_space=pltpu.HBM)] * 7,
        out_specs=pl.BlockSpec(memory_space=pl.ANY),
        scratch_shapes=scratch,
        compiler_params=pltpu.CompilerParams(collective_id=0, has_side_effects=True, vmem_limit_bytes=32 << 20),
    )(*(
        pltpu.with_memory_space_constraint(x, pltpu.HBM)
        for x in (radiation, phases, energy, pixels, destination, propagator, transmit)
    ))


def solution(mesh):
    sizes = dict(mesh.shape)
    return jax.shard_map(
        functools.partial(on_device, sizes["cuts"], sizes["group"]),
        mesh=mesh,
        in_specs=(
            P(("cuts", "group"), None, None, None),
            P(("cuts", "group"), None, None),
            P(("cuts", "group"), None, None),
            P(("cuts", "group"), None, None),
            P(("cuts", "group"), None),
            P(),
            P(),
        ),
        out_specs=P(("cuts", "group"), None, None, None),
        check_vma=False,
    )
```

```python
import contextlib
import functools
import math

import jax
import jax.numpy as jnp
from jax import lax
from jax.experimental import pallas as pl
from jax.experimental.pallas import tpu as pltpu
from jax.sharding import PartitionSpec as P

KICK_RATE = 0.5
PHASE_RATE = 1.0
EMIT_RATE = 0.5
F32 = jnp.float32
BF16 = jnp.bfloat16
MESH = pl.DeviceIdType.MESH
ROWS = 8
HALF = 4


def tag(name):
    return contextlib.nullcontext()


def iota(shape, dim):
    return lax.broadcasted_iota(jnp.int32, shape, dim)


def split(x):
    high = x.astype(BF16)
    return high, (x - high.astype(F32)).astype(BF16)


def dot(a, b):
    return jnp.dot(a, b, preferred_element_type=F32)


def dot_nt(a, b):
    return lax.dot_general(a, b, (((1,), (1,)), ((), ())), preferred_element_type=F32)


def dot_exact(a, b):
    return jnp.dot(a, b, precision=lax.Precision.HIGHEST, preferred_element_type=F32)


def turns(product, total):
    whole = jnp.floor((product + 0.5) * (1.0 / total))
    angle = (product - whole * total) * (2.0 * math.pi / total)
    return jnp.cos(angle), jnp.sin(angle)


def stack2(a, b, c, d):
    return jnp.concatenate(
        [jnp.concatenate([a, b], axis=1), jnp.concatenate([c, d], axis=1)], axis=0
    )


def triple(matrix):
    high, low = split(matrix)
    return jnp.concatenate([high, high, low], axis=1)


def apply_triple(packed, data):
    high, low = split(data)
    return dot(packed, jnp.concatenate([high, low, high], axis=0))


def kernel(
    n_cuts, n_group, grid, blocks, width,
    radiation, phases, energy, pixels, destination, propagator, transmit,
    out,
    phase_in, power_in, pixel_in, target_in, prop_in, gain_in,
    field, prop_hi, prop_lo, cut_fwd, cut_inv, mid_op,
    slip_a, got_a, slip_p, got_p, slip_b, got_b,
    hot_now, hot_next, turned_now, turned_next, row_now, row_next, read, weight, source,
    send1, recv1, send2, recv2, send3, recv3, send4, recv4, send_e, recv_e, send_x, recv_x,
    go_sem, load_sems, send_sems, recv_sems,
):
    c = lax.axis_index("cuts")
    g = lax.axis_index("group")
    total = n_cuts * n_group
    me = c * n_group + g
    n_active = grid // ROWS
    third = c // 3
    lane = c - 3 * third
    active = lane != 1
    idle = jnp.logical_not(active)
    side = lane // 2
    idle_cut = c - lane + 1
    half_group = n_group // 2
    my_active = 2 * third + side
    owner = jnp.where(active, c, c - 1 + 2 * (g // half_group))
    unit = jnp.where(active, g, n_group + g % half_group)
    many = 2 * n_cuts

    def wrap(value, size):
        return jnp.where(value >= size, value - size, value)

    def device(offset):
        other = wrap(me + (offset + total if offset < 0 else offset), total)
        return other // n_group, other % n_group

    def repeat(count, body):
        def step(i, carry):
            body(i)
            return carry
        lax.fori_loop(0, count, step, 0, unroll=math.gcd(count, 4))

    loads = [
        pltpu.make_async_copy(src, dst, load_sems.at[i])
        for i, (src, dst) in enumerate([
            (pixels.at[0], pixel_in), (radiation.at[0, 0], field.at[pl.ds(0, grid)]),
            (radiation.at[0, 1], field.at[pl.ds(grid, grid)]), (phases.at[0], phase_in),
            (energy.at[0], power_in), (destination, target_in), (propagator, prop_in), (transmit, gain_in),
        ])
    ]
    for load in loads:
        load.start()
    barrier = pltpu.get_barrier_semaphore()

    def hello(cc, gg):
        pl.semaphore_signal(barrier, inc=1, device_id=(cc, gg), device_id_type=MESH)

    ahead_group = wrap(g + 3, n_group)
    behind_group = wrap(g + n_group - 3, n_group)
    ring = n_cuts // 2
    cut_order = sorted(range(n_cuts), key=lambda j: -min(j % ring, ring - j % ring))
    quads = n_group // 4
    quad_order = sorted(range(quads), key=lambda j: -min(j, quads - j))
    quad = g // 4
    for j in cut_order:
        cut = wrap(c + j, n_cuts)
        hello(cut, ahead_group)
        hello(cut, behind_group)
        if j:
            hello(cut, g)
    hello(*device(-1))
    hello(*device(1))

    @pl.when(active)
    def _():
        repeat(n_group - 1, lambda i: hello(c, wrap(g + 1 + i, n_group)))
        repeat(half_group, lambda i: hello(idle_cut, half_group * side + i))

    @pl.when(idle)
    def _():
        repeat(n_group, lambda i: hello(owner, wrap(g + i, n_group)))

    def meet():
        greeted = 2 + n_cuts - 1 + 2 * n_cuts

        @pl.when(active)
        def _():
            pl.semaphore_wait(barrier, greeted + n_group - 1 + half_group)

        @pl.when(idle)
        def _():
            pl.semaphore_wait(barrier, greeted + n_group)

    def remote(stage, src, dst, cc, gg):
        return pltpu.make_async_remote_copy(
            src_ref=src, dst_ref=dst, send_sem=send_sems.at[stage], recv_sem=recv_sems.at[stage],
            device_id=(cc, gg), device_id_type=MESH,
        )

    def keep(stage, src, dst):
        pltpu.make_async_copy(src, dst, recv_sems.at[stage]).start()

    def push(mine, stage, src, dst, cc, gg):
        @pl.when(mine)
        def _():
            keep(stage, src, dst)

        @pl.when(jnp.logical_not(mine))
        def _():
            remote(stage, src, dst, cc, gg).start()

    def arrived(stage, ref):
        with tag("wait%d" % stage):
            remote(stage, ref, ref, c, g).wait_recv()

    def sent(stage, ref):
        remote(stage, ref, ref, c, g).wait_send()

    def tile(ref, index, rows=8):
        return ref.at[pl.ds(pl.multiple_of(index * 8, 8), rows)]

    shift = grid.bit_length()
    pairs = grid // 2
    places = 2 * grid

    def low_rows(value, size):
        packed = jnp.broadcast_to(value, (16, width)).astype(BF16)
        return jnp.broadcast_to(packed[None], (size // 16, 16, width)).reshape(size, width)

    def mark(count, cells, hot, rows, turned):
        rows[:count] = lax.shift_right_arithmetic(cells, shift)
        place = (cells & (places - 1)).astype(F32)
        spots = iota((places, width), 0).astype(F32).astype(BF16)
        one, zero = jnp.ones((places, width), BF16), jnp.zeros((places, width), BF16)
        for b in range(count):
            hot[:, b * width:(b + 1) * width] = jnp.where(spots == low_rows(place[b:b + 1], places), one, zero)
        columns = jnp.transpose(place)
        spots = iota((width, grid), 1).astype(F32).astype(BF16)
        one, zero = jnp.ones((width, grid), BF16), jnp.zeros((width, grid), BF16)
        for b in range(count):
            column = jnp.broadcast_to(columns[:, b:b + 1], (width, grid))
            for q in range(2):
                match = spots == (column - float(q * grid)).astype(BF16)
                turned[b * width:(b + 1) * width, q * grid:(q + 1) * grid] = jnp.where(match, one, zero)

    def look(count, hot, rows):
        low = jnp.concatenate([field[pl.ds(0, grid, stride=2), :], field[pl.ds(1, grid, stride=2), :]], axis=1).astype(BF16)
        real, imag = [], []
        for two in range(count // 2):
            picked = dot(low, hot[:, two * 2 * width:(two + 1) * 2 * width])
            for b in range(2):
                at = rows[2 * two + b:2 * two + b + 1]
                match = iota((pairs, width), 0) == jnp.broadcast_to(at, (pairs, width))
                part = picked[:, b * width:(b + 1) * width]
                real.append(jnp.sum(jnp.where(match, part[:pairs], 0.0), axis=0, keepdims=True))
                imag.append(jnp.sum(jnp.where(match, part[pairs:], 0.0), axis=0, keepdims=True))
        read[0, :count] = jnp.concatenate(real, axis=0)
        read[1, :count] = jnp.concatenate(imag, axis=0)

    def kick(count, phase, power, cos, sin):
        power = power - KICK_RATE * (read[0, :count] * cos - read[1, :count] * sin)
        phase = phase + PHASE_RATE * power
        weight[0, :count] = jnp.cos(phase)
        weight[1, :count] = -jnp.sin(phase)
        return phase, power

    def deposit(count, rows, turned):
        chunk = 8 if count % 8 == 0 else count
        gathered = jnp.zeros((grid, places), F32)
        spots = iota((pairs, width), 0).astype(F32).astype(BF16)
        zero = jnp.zeros((pairs, width), BF16)
        for first in range(0, count, chunk):
            tops, bottoms = [], []
            for b in range(first, first + chunk):
                match = spots == low_rows(rows[b:b + 1].astype(F32), pairs)
                tops.append(jnp.where(match, low_rows(weight[0, b:b + 1], pairs), zero))
                bottoms.append(jnp.where(match, low_rows(weight[1, b:b + 1], pairs), zero))
            spread = jnp.concatenate([jnp.concatenate(tops, axis=1), jnp.concatenate(bottoms, axis=1)], axis=0)
            gathered = gathered + dot(spread, turned[first * width:(first + chunk) * width])
        source[...] = gathered

    def emit():
        field[pl.ds(0, grid, stride=2), :] = field[pl.ds(0, grid, stride=2), :] + EMIT_RATE * source[:, :grid]
        field[pl.ds(1, grid, stride=2), :] = field[pl.ds(1, grid, stride=2), :] + EMIT_RATE * source[:, grid:]

    def diffract(keep):
        emit()
        high, low = split(field[...])
        both = dot(prop_hi[...], jnp.concatenate([high, low], axis=1))
        left = both[:, :grid] + both[:, grid:] + dot(prop_lo[...], high)
        left = jnp.concatenate([left[:grid], left[grid:]], axis=1)
        high, low = split(left)
        result = dot_nt(high, prop_hi[...]) + dot_nt(low, prop_hi[...]) + dot_nt(high, prop_lo[...])
        return jnp.where(keep, result, 0.0)

    def set_field(result):
        field[:grid] = result[:, :grid]
        field[grid:] = result[:, grid:]

    loads[0].wait()
    mark(blocks, pixel_in[...], hot_now, row_now, turned_now)
    for load in loads[1:]:
        load.wait()
    look(blocks, hot_now, row_now)
    phase = phase_in[...]
    phase, power = kick(blocks, phase, power_in[...], jnp.cos(phase), jnp.sin(phase))
    slip_a[:blocks] = phase
    slip_a[blocks:2 * blocks] = power
    slip_a[2 * blocks:3 * blocks] = pixel_in[...].astype(F32)
    slip_a[3 * blocks:] = jnp.zeros_like(slip_a[3 * blocks:])
    slip_a[3 * blocks:3 * blocks + 1, :blocks] = target_in[...].astype(F32)
    with tag("meet"):
        meet()
    remote(0, slip_a, got_a, *device(-1)).start()
    prop = stack2(prop_in[0], -prop_in[1], prop_in[1], prop_in[0])
    high, low = split(prop)
    prop_hi[...] = high
    prop_lo[...] = low
    deposit(blocks, row_now, turned_now)
    set_field(diffract(me != total - 1))

    arrived(0, got_a)
    mark(blocks, got_a[2 * blocks:3 * blocks].astype(jnp.int32), hot_now, row_now, turned_now)
    look(blocks, hot_now, row_now)
    phase = got_a[:blocks]
    phase, power = kick(blocks, phase, got_a[blocks:2 * blocks], jnp.cos(phase), jnp.sin(phase))
    deposit(blocks, row_now, turned_now)
    result = diffract(me != total - 2)
    for a in range(n_active):
        for h in range(2):
            at = a * ROWS + h * HALF
            send1[h, a * 8:a * 8 + HALF] = result[at:at + HALF, :grid]
            send1[h, a * 8 + HALF:(a + 1) * 8] = result[at:at + HALF, grid:]

    for j in cut_order:
        cut = wrap(c + j, n_cuts)
        row = (cut * 43) >> 7
        place = cut - 3 * row

        @pl.when(place != 1)
        def _():
            a = 2 * row + (place >> 1)
            for h in range(2):
                if j:
                    remote(1 + h, tile(send1.at[h], a), tile(recv1.at[h], c), cut, g).start()
                else:
                    keep(1 + h, tile(send1.at[h], a), tile(recv1.at[h], c))

    target = got_a[3 * blocks:3 * blocks + 1, :blocks]
    square = (blocks, blocks)
    wide = jnp.broadcast_to(target, square)
    tall = jnp.sum(jnp.where(iota(square, 0) == iota(square, 1), wide, 0.0), axis=1, keepdims=True)
    same = jnp.logical_and(jnp.broadcast_to(tall, square) == wide, iota(square, 0) < iota(square, 1))
    rank = jnp.sum(jnp.where(same, 1.0, 0.0), axis=0, keepdims=True)
    payload = jnp.concatenate([phase, power, got_a[2 * blocks:3 * blocks] + 1.0], axis=1)
    shape = (n_cuts, blocks)
    goes = jnp.broadcast_to(target, shape) == iota(shape, 0).astype(F32)
    for slot in range(2):
        pick = jnp.logical_and(goes, jnp.broadcast_to(rank, shape) == float(slot))
        moved = dot_exact(jnp.where(pick, 1.0, 0.0), payload)
        for part in range(2):
            send_e[pl.ds(slot * 2 + part, n_cuts, stride=8), :] = moved[:, part * width:(part + 1) * width]
        send_x[pl.ds(slot, n_cuts, stride=8), :] = moved[:, 2 * width:]
    carry_cut = jnp.where(jnp.logical_and(g >= n_group - 3, g <= n_group - 2), 1, 0)

    def send_electrons(stage, rows, src, dst):
        for j in cut_order:
            cut = wrap(c + j, n_cuts)
            k = wrap(cut + n_cuts - carry_cut, n_cuts)
            remote(stage, tile(src, k, rows), tile(dst, c, rows), cut, ahead_group).start()

    with tag("sendx"):
        send_electrons(10, 2, send_x, recv_x)

    shape = (n_cuts, n_cuts)
    g_real = g.astype(F32)
    cos, sin = turns((iota(shape, 1).astype(F32) * n_group + g_real) * iota(shape, 0).astype(F32), total)
    cut_fwd[...] = triple(stack2(cos, sin, -sin, cos))
    cos, sin = turns((iota(shape, 0).astype(F32) * n_group + g_real) * iota(shape, 1).astype(F32), total)
    cut_inv[...] = triple(stack2(cos, -sin, sin, cos))
    first_freq = unit // 2
    shape = (n_group, total)
    chosen = iota(shape, 1) == first_freq + n_cuts * iota(shape, 0)
    gain_real = jnp.sum(jnp.where(chosen, jnp.broadcast_to(gain_in[0:1], shape), 0.0), axis=1, keepdims=True)
    gain_imag = jnp.sum(jnp.where(chosen, jnp.broadcast_to(gain_in[1:2], shape), 0.0), axis=1, keepdims=True)
    shape = (n_group, n_group)
    lag_cos, lag_sin = turns((first_freq.astype(F32) + n_cuts * iota(shape, 0).astype(F32)) * 4.0, total)
    scale = 1.0 / total
    turn_real = (gain_real * lag_cos + gain_imag * lag_sin) * scale
    turn_imag = (gain_imag * lag_cos - gain_real * lag_sin) * scale
    cos, sin = turns(iota(shape, 0).astype(F32) * iota(shape, 1).astype(F32), n_group)
    shaped_real = turn_real * cos + turn_imag * sin
    shaped_imag = turn_imag * cos - turn_real * sin
    mid_op[...] = triple(dot_exact(
        stack2(cos, -sin, sin, cos), stack2(shaped_real, -shaped_imag, shaped_imag, shaped_real)
    ))

    def apply(operator, count, source_ref, target_ref):
        real = [source_ref[pl.ds(j, count, stride=8), :] for j in range(HALF)]
        imag = [source_ref[pl.ds(HALF + j, count, stride=8), :] for j in range(HALF)]
        data = jnp.concatenate([jnp.concatenate(real, axis=1), jnp.concatenate(imag, axis=1)], axis=0)
        done = apply_triple(operator[...], data)
        for j in range(HALF):
            target_ref[pl.ds(j, count, stride=8), :] = done[:count, j * grid:(j + 1) * grid]
            target_ref[pl.ds(HALF + j, count, stride=8), :] = done[count:, j * grid:(j + 1) * grid]

    @pl.when(active)
    def _():
        for h in range(2):
            arrived(1 + h, recv1.at[h])
            with tag("fwd%d" % h):
                apply(cut_fwd, n_cuts, recv1.at[h], send2.at[h])
        with tag("send2"):
            for j in quad_order:
                y = wrap(quad + j, quads)
                for r in range(4):
                    src, dst = tile(send2.at[r % 2], 2 * y + r // 2), tile(recv2, g)
                    if j:
                        remote(3, src, dst, c, 4 * y + r).start()
                    else:
                        push(4 * y + r == g, 3, src, dst, c, 4 * y + r)
                low = y - side * (quads // 2)

                @pl.when(jnp.logical_and(low >= 0, low < quads // 2))
                def _():
                    for r in range(4):
                        src = tile(send2.at[r % 2], n_group // 2 + 2 * low + r // 2)
                        remote(3, src, tile(recv2, g), idle_cut, 4 * y + r).start()

    @pl.when(active)
    def _():
        @pl.when(side == g // half_group)
        def _():
            pl.semaphore_signal(go_sem, inc=1, device_id=(idle_cut, g), device_id_type=MESH)

    @pl.when(idle)
    def _():
        with tag("go"):
            pl.semaphore_wait(go_sem, 1)

    with tag("sende"):
        send_electrons(9, 4, send_e, recv_e)

    arrived(3, recv2)
    with tag("mid"):
        apply(mid_op, n_group, recv2, send3)

    for h in range(2):
        @pl.when((unit & 1) == h)
        def _():
            with tag("send3"):
                for j in quad_order:
                    y = wrap(quad + j, quads)
                    for r in range(4):
                        src, dst = tile(send3, 4 * y + r), tile(recv3.at[h], unit >> 1)
                        if j:
                            remote(4 + h, src, dst, owner, 4 * y + r).start()
                        else:
                            push(jnp.logical_and(active, 4 * y + r == g), 4 + h, src, dst, owner, 4 * y + r)

    arrived(10, recv_x.at[pl.ds(0, n_cuts * 2)])

    def cells_of(value):
        return (value + 0.25).astype(jnp.int32) - 1

    cells = jnp.concatenate([recv_x[pl.ds(0, n_cuts, stride=8), :], recv_x[pl.ds(1, n_cuts, stride=8), :]], axis=0)
    slip_p[...] = cells
    remote(11, slip_p, got_p, *device(-1)).start()
    with tag("mark3"):
        mark(many, cells_of(cells), hot_now, row_now, turned_now)

    @pl.when(active)
    def _():
        for h in range(2):
            arrived(4 + h, recv3.at[h])
            with tag("inv%d" % h):
                apply(cut_inv, n_cuts, recv3.at[h], send4.at[h])
        with tag("send4"):
            for j in cut_order:
                cut = wrap(c + j, n_cuts)
                for h in range(2):
                    src, dst = tile(send4.at[h], cut), tile(recv4.at[h], my_active)
                    if j:
                        remote(6 + h, src, dst, cut, g).start()
                    else:
                        keep(6 + h, src, dst)

    arrived(11, got_p)
    with tag("mark4"):
        mark(many, cells_of(got_p[...]), hot_next, row_next, turned_next)
    arrived(9, recv_e.at[pl.ds(0, n_cuts * 4)])

    def pieces(part):
        return jnp.concatenate(
            [recv_e[pl.ds(part, n_cuts, stride=8), :], recv_e[pl.ds(2 + part, n_cuts, stride=8), :]], axis=0
        )

    phase = pieces(0)
    cos, sin = jnp.cos(phase), jnp.sin(phase)
    for h in range(2):
        arrived(6 + h, recv4.at[h])
        for a in range(n_active):
            at = a * ROWS + h * HALF
            field[at:at + HALF] = recv4[h, a * 8:a * 8 + HALF]
            field[grid + at:grid + at + HALF] = recv4[h, a * 8 + HALF:(a + 1) * 8]

    with tag("look3"):
        look(many, hot_now, row_now)
    with tag("kick3"):
        phase, power = kick(many, phase, pieces(1), cos, sin)
        slip_b[:many] = phase
        slip_b[many:] = power
    remote(12, slip_b, got_b, *device(-1)).start()
    with tag("deposit3"):
        deposit(many, row_now, turned_now)
    with tag("diffract3"):
        set_field(diffract(me != 1))

    with tag("look4"):
        look(many, hot_next, row_next)
    arrived(12, got_b)
    with tag("kick4"):
        phase = got_b[:many]
        kick(many, phase, got_b[many:], jnp.cos(phase), jnp.sin(phase))
    with tag("deposit4"):
        deposit(many, row_next, turned_next)
    with tag("diffract4"):
        result = diffract(me != 0)
        out[0, 0] = result[:, :grid]
        out[0, 1] = result[:, grid:]

    sent(0, slip_a)
    sent(9, send_e.at[pl.ds(0, n_cuts * 4)])
    sent(10, send_x.at[pl.ds(0, n_cuts * 2)])
    sent(11, slip_p)
    sent(12, slip_b)

    @pl.when(active)
    def _():
        for h in range(2):
            sent(1 + h, send1.at[h, pl.ds(0, (n_active - 1) * 8)])
            sent(6 + h, send4.at[h, pl.ds(0, (n_cuts - 1) * 8)])
        for h in range(2):
            @pl.when((unit & 1) == h)
            def _():
                sent(4 + h, send3.at[pl.ds(0, (n_group - 1) * 8)])
        sent(3, send2.at[0])
        sent(3, send2.at[1, pl.ds(0, (n_cuts - 1) * 8)])

    @pl.when(idle)
    def _():
        for h in range(2):
            sent(1 + h, send1.at[h])
            @pl.when((unit & 1) == h)
            def _():
                sent(4 + h, send3)


def on_device(n_cuts, n_group, radiation, phases, energy, pixels, destination, propagator, transmit):
    grid = radiation.shape[-1]
    blocks, width = phases.shape[1:]
    many = 2 * n_cuts
    n_active = grid // ROWS
    vmem = lambda shape, kind=F32: pltpu.VMEM(shape, kind)
    scratch = [
        vmem((blocks, width)), vmem((blocks, width)), vmem((blocks, width), jnp.int32),
        vmem(destination.shape, jnp.int32), vmem(propagator.shape), vmem(transmit.shape),
        vmem((2 * grid, grid)),
        vmem((2 * grid, 2 * grid), BF16), vmem((2 * grid, 2 * grid), BF16),
        vmem((2 * n_cuts, 6 * n_cuts), BF16), vmem((2 * n_cuts, 6 * n_cuts), BF16),
        vmem((2 * n_group, 6 * n_group), BF16),
        vmem((3 * blocks + 8, width)), vmem((3 * blocks + 8, width)),
        vmem((many, width)), vmem((many, width)),
        vmem((2 * many, width)), vmem((2 * many, width)),
        vmem((2 * grid, many * width), BF16), vmem((2 * grid, many * width), BF16),
        vmem((many * width, 2 * grid), BF16), vmem((many * width, 2 * grid), BF16),
        vmem((many, width), jnp.int32), vmem((many, width), jnp.int32),
        vmem((2, many, width)), vmem((2, many, width)),
        vmem((grid, 2 * grid)),
        vmem((2, n_active * 8, grid)), vmem((2, n_cuts * 8, grid)),
        vmem((2, n_cuts * 8, grid)), vmem((n_group * 8, grid)),
        vmem((n_group * 8, grid)), vmem((2, n_cuts * 8, grid)),
        vmem((2, n_cuts * 8, grid)), vmem((2, n_active * 8, grid)),
        vmem((n_cuts * 8, width)), vmem((n_cuts * 8, width)), vmem((n_cuts * 8, width)), vmem((n_cuts * 8, width)),
        pltpu.SemaphoreType.REGULAR, pltpu.SemaphoreType.DMA((8,)), pltpu.SemaphoreType.DMA((13,)), pltpu.SemaphoreType.DMA((13,)),
    ]
    return pl.pallas_call(
        functools.partial(kernel, n_cuts, n_group, grid, blocks, width),
        out_shape=jax.ShapeDtypeStruct(radiation.shape, F32),
        in_specs=[pl.BlockSpec(memory_space=pltpu.HBM)] * 7,
        out_specs=pl.BlockSpec(memory_space=pltpu.VMEM),
        scratch_shapes=scratch,
        compiler_params=pltpu.CompilerParams(collective_id=0, has_side_effects=True, vmem_limit_bytes=32 << 20),
    )(*(
        pltpu.with_memory_space_constraint(x, pltpu.HBM)
        for x in (radiation, phases, energy, pixels, destination, propagator, transmit)
    ))


def solution(mesh):
    sizes = dict(mesh.shape)
    return jax.shard_map(
        functools.partial(on_device, sizes["cuts"], sizes["group"]),
        mesh=mesh,
        in_specs=(
            P(("cuts", "group"), None, None, None),
            P(("cuts", "group"), None, None),
            P(("cuts", "group"), None, None),
            P(("cuts", "group"), None, None),
            P(("cuts", "group"), None),
            P(),
            P(),
        ),
        out_specs=P(("cuts", "group"), None, None, None),
        check_vma=False,
    )
```

```python
import contextlib
import functools
import math

import jax
import jax.numpy as jnp
from jax import lax
from jax.experimental import pallas as pl
from jax.experimental.pallas import tpu as pltpu
from jax.sharding import PartitionSpec as P

KICK_RATE = 0.5
PHASE_RATE = 1.0
EMIT_RATE = 0.5
F32 = jnp.float32
BF16 = jnp.bfloat16
MESH = pl.DeviceIdType.MESH
ROWS = 8
HALF = 4


def tag(name):
    return contextlib.nullcontext()


def iota(shape, dim):
    return lax.broadcasted_iota(jnp.int32, shape, dim)


def split(x):
    high = x.astype(BF16)
    return high, (x - high.astype(F32)).astype(BF16)


def dot(a, b):
    return jnp.dot(a, b, preferred_element_type=F32)


def dot_nt(a, b):
    return lax.dot_general(a, b, (((1,), (1,)), ((), ())), preferred_element_type=F32)


def dot_exact(a, b):
    return jnp.dot(a, b, precision=lax.Precision.HIGHEST, preferred_element_type=F32)


def turns(product, total):
    whole = jnp.floor((product + 0.5) * (1.0 / total))
    angle = (product - whole * total) * (2.0 * math.pi / total)
    return jnp.cos(angle), jnp.sin(angle)


def stack2(a, b, c, d):
    return jnp.concatenate(
        [jnp.concatenate([a, b], axis=1), jnp.concatenate([c, d], axis=1)], axis=0
    )


def triple(matrix):
    high, low = split(matrix)
    return jnp.concatenate([high, high, low], axis=1)


def apply_triple(packed, data):
    high, low = split(data)
    return dot(packed, jnp.concatenate([high, low, high], axis=0))


def kernel(
    n_cuts, n_group, grid, blocks, width,
    radiation, phases, energy, pixels, destination, propagator, transmit,
    out,
    phase_in, power_in, pixel_in, target_in, prop_in, gain_in,
    field, prop_hi, prop_lo, cut_fwd, cut_inv, mid_op,
    slip_a, got_a, slip_p, got_p, slip_b, got_b,
    hot_now, hot_next, turned_now, turned_next, row_now, row_next, read, weight, source,
    send1, recv1, send2, recv2, send3, recv3, send4, recv4, send_e, recv_e, send_x, recv_x,
    go_sem, load_sems, send_sems, recv_sems,
):
    c = lax.axis_index("cuts")
    g = lax.axis_index("group")
    total = n_cuts * n_group
    me = c * n_group + g
    n_active = grid // ROWS
    third = c // 3
    lane = c - 3 * third
    active = lane != 1
    idle = jnp.logical_not(active)
    side = lane // 2
    idle_cut = c - lane + 1
    half_group = n_group // 2
    my_active = 2 * third + side
    owner = jnp.where(active, c, c - 1 + 2 * (g // half_group))
    unit = jnp.where(active, g, n_group + g % half_group)
    many = 2 * n_cuts

    def wrap(value, size):
        return jnp.where(value >= size, value - size, value)

    def device(offset):
        other = wrap(me + (offset + total if offset < 0 else offset), total)
        return other // n_group, other % n_group

    def repeat(count, body):
        def step(i, carry):
            body(i)
            return carry
        lax.fori_loop(0, count, step, 0, unroll=math.gcd(count, 4))

    loads = [
        pltpu.make_async_copy(src, dst, load_sems.at[i])
        for i, (src, dst) in enumerate([
            (pixels.at[0], pixel_in), (radiation.at[0, 0], field.at[pl.ds(0, grid)]),
            (radiation.at[0, 1], field.at[pl.ds(grid, grid)]), (phases.at[0], phase_in),
            (energy.at[0], power_in), (destination, target_in), (propagator, prop_in), (transmit, gain_in),
        ])
    ]
    for load in loads:
        load.start()
    barrier = pltpu.get_barrier_semaphore()

    def hello(cc, gg):
        pl.semaphore_signal(barrier, inc=1, device_id=(cc, gg), device_id_type=MESH)

    ahead_group = wrap(g + 3, n_group)
    behind_group = wrap(g + n_group - 3, n_group)
    ring = n_cuts // 2
    cut_order = sorted(range(n_cuts), key=lambda j: -min(j % ring, ring - j % ring))
    quads = n_group // 4
    quad_order = sorted(range(quads), key=lambda j: -min(j, quads - j))
    quad = g // 4
    for j in cut_order:
        cut = wrap(c + j, n_cuts)
        hello(cut, ahead_group)
        hello(cut, behind_group)
        if j:
            hello(cut, g)
    hello(*device(-1))
    hello(*device(1))

    @pl.when(active)
    def _():
        repeat(n_group - 1, lambda i: hello(c, wrap(g + 1 + i, n_group)))
        repeat(half_group, lambda i: hello(idle_cut, half_group * side + i))

    @pl.when(idle)
    def _():
        repeat(n_group, lambda i: hello(owner, wrap(g + i, n_group)))

    def meet():
        greeted = 2 + n_cuts - 1 + 2 * n_cuts

        @pl.when(active)
        def _():
            pl.semaphore_wait(barrier, greeted + n_group - 1 + half_group)

        @pl.when(idle)
        def _():
            pl.semaphore_wait(barrier, greeted + n_group)

    def remote(stage, src, dst, cc, gg):
        return pltpu.make_async_remote_copy(
            src_ref=src, dst_ref=dst, send_sem=send_sems.at[stage], recv_sem=recv_sems.at[stage],
            device_id=(cc, gg), device_id_type=MESH,
        )

    def keep(stage, src, dst):
        pltpu.make_async_copy(src, dst, recv_sems.at[stage]).start()

    def push(mine, stage, src, dst, cc, gg):
        @pl.when(mine)
        def _():
            keep(stage, src, dst)

        @pl.when(jnp.logical_not(mine))
        def _():
            remote(stage, src, dst, cc, gg).start()

    def arrived(stage, ref):
        with tag("wait%d" % stage):
            remote(stage, ref, ref, c, g).wait_recv()

    def sent(stage, ref):
        remote(stage, ref, ref, c, g).wait_send()

    def tile(ref, index, rows=8):
        return ref.at[pl.ds(pl.multiple_of(index * 8, 8), rows)]

    shift = grid.bit_length()
    pairs = grid // 2
    places = 2 * grid

    def alone(piece):
        pl.when(me >= 0)(piece)

    def low_rows(value, size):
        packed = jnp.broadcast_to(value, (16, width)).astype(BF16)
        return jnp.broadcast_to(packed[None], (size // 16, 16, width)).reshape(size, width)

    def mark(count, cells, hot, rows, turned):
        rows[:count] = lax.shift_right_arithmetic(cells, shift)
        place = (cells & (places - 1)).astype(F32)
        spots = iota((places, width), 0).astype(F32).astype(BF16)
        one, zero = jnp.ones((places, width), BF16), jnp.zeros((places, width), BF16)
        for b in range(count):
            hot[:, b * width:(b + 1) * width] = jnp.where(spots == low_rows(place[b:b + 1], places), one, zero)
        columns = jnp.transpose(place)
        spots = iota((width, grid), 1).astype(F32).astype(BF16)
        one, zero = jnp.ones((width, grid), BF16), jnp.zeros((width, grid), BF16)
        for b in range(count):
            column = jnp.broadcast_to(columns[:, b:b + 1], (width, grid))
            for q in range(2):
                match = spots == (column - float(q * grid)).astype(BF16)
                turned[b * width:(b + 1) * width, q * grid:(q + 1) * grid] = jnp.where(match, one, zero)

    def look(count, hot, rows):
        low = jnp.concatenate([field[pl.ds(0, grid, stride=2), :], field[pl.ds(1, grid, stride=2), :]], axis=1).astype(BF16)
        real, imag = [], []
        for two in range(count // 2):
            picked = dot(low, hot[:, two * 2 * width:(two + 1) * 2 * width])
            for b in range(2):
                at = rows[2 * two + b:2 * two + b + 1]
                match = iota((pairs, width), 0) == jnp.broadcast_to(at, (pairs, width))
                part = picked[:, b * width:(b + 1) * width]
                real.append(jnp.sum(jnp.where(match, part[:pairs], 0.0), axis=0, keepdims=True))
                imag.append(jnp.sum(jnp.where(match, part[pairs:], 0.0), axis=0, keepdims=True))
        read[0, :count] = jnp.concatenate(real, axis=0)
        read[1, :count] = jnp.concatenate(imag, axis=0)

    def kick(count, phase, power, cos, sin):
        power = power - KICK_RATE * (read[0, :count] * cos - read[1, :count] * sin)
        phase = phase + PHASE_RATE * power
        weight[0, :count] = jnp.cos(phase)
        weight[1, :count] = -jnp.sin(phase)
        return phase, power

    def deposit(count, rows, turned):
        chunk = 8 if count % 8 == 0 else count
        gathered = jnp.zeros((grid, places), F32)
        spots = iota((pairs, width), 0).astype(F32).astype(BF16)
        zero = jnp.zeros((pairs, width), BF16)
        for first in range(0, count, chunk):
            tops, bottoms = [], []
            for b in range(first, first + chunk):
                match = spots == low_rows(rows[b:b + 1].astype(F32), pairs)
                tops.append(jnp.where(match, low_rows(weight[0, b:b + 1], pairs), zero))
                bottoms.append(jnp.where(match, low_rows(weight[1, b:b + 1], pairs), zero))
            spread = jnp.concatenate([jnp.concatenate(tops, axis=1), jnp.concatenate(bottoms, axis=1)], axis=0)
            gathered = gathered + dot(spread, turned[first * width:(first + chunk) * width])
        source[...] = gathered

    def emit():
        field[pl.ds(0, grid, stride=2), :] = field[pl.ds(0, grid, stride=2), :] + EMIT_RATE * source[:, :grid]
        field[pl.ds(1, grid, stride=2), :] = field[pl.ds(1, grid, stride=2), :] + EMIT_RATE * source[:, grid:]

    def diffract(keep):
        emit()
        high, low = split(field[...])
        both = dot(prop_hi[...], jnp.concatenate([high, low], axis=1))
        left = both[:, :grid] + both[:, grid:] + dot(prop_lo[...], high)
        left = jnp.concatenate([left[:grid], left[grid:]], axis=1)
        high, low = split(left)
        result = dot_nt(high, prop_hi[...]) + dot_nt(low, prop_hi[...]) + dot_nt(high, prop_lo[...])
        return jnp.where(keep, result, 0.0)

    def set_field(result):
        field[:grid] = result[:, :grid]
        field[grid:] = result[:, grid:]

    loads[0].wait()
    mark(blocks, pixel_in[...], hot_now, row_now, turned_now)
    for load in loads[1:]:
        load.wait()
    look(blocks, hot_now, row_now)
    phase = phase_in[...]
    phase, power = kick(blocks, phase, power_in[...], jnp.cos(phase), jnp.sin(phase))
    slip_a[:blocks] = phase
    slip_a[blocks:2 * blocks] = power
    slip_a[2 * blocks:3 * blocks] = pixel_in[...].astype(F32)
    slip_a[3 * blocks:] = jnp.zeros_like(slip_a[3 * blocks:])
    slip_a[3 * blocks:3 * blocks + 1, :blocks] = target_in[...].astype(F32)
    with tag("meet"):
        meet()
    remote(0, slip_a, got_a, *device(-1)).start()
    prop = stack2(prop_in[0], -prop_in[1], prop_in[1], prop_in[0])
    high, low = split(prop)
    prop_hi[...] = high
    prop_lo[...] = low
    alone(lambda: deposit(blocks, row_now, turned_now))
    set_field(diffract(me != total - 1))

    arrived(0, got_a)
    mark(blocks, got_a[2 * blocks:3 * blocks].astype(jnp.int32), hot_now, row_now, turned_now)
    look(blocks, hot_now, row_now)
    phase = got_a[:blocks]
    phase, power = kick(blocks, phase, got_a[blocks:2 * blocks], jnp.cos(phase), jnp.sin(phase))
    alone(lambda: deposit(blocks, row_now, turned_now))
    result = diffract(me != total - 2)
    for a in range(n_active):
        for h in range(2):
            at = a * ROWS + h * HALF
            send1[h, a * 8:a * 8 + HALF] = result[at:at + HALF, :grid]
            send1[h, a * 8 + HALF:(a + 1) * 8] = result[at:at + HALF, grid:]

    for j in cut_order:
        cut = wrap(c + j, n_cuts)
        row = (cut * 43) >> 7
        place = cut - 3 * row

        @pl.when(place != 1)
        def _():
            a = 2 * row + (place >> 1)
            for h in range(2):
                if j:
                    remote(1 + h, tile(send1.at[h], a), tile(recv1.at[h], c), cut, g).start()
                else:
                    keep(1 + h, tile(send1.at[h], a), tile(recv1.at[h], c))

    target = got_a[3 * blocks:3 * blocks + 1, :blocks]
    square = (blocks, blocks)
    wide = jnp.broadcast_to(target, square)
    tall = jnp.sum(jnp.where(iota(square, 0) == iota(square, 1), wide, 0.0), axis=1, keepdims=True)
    same = jnp.logical_and(jnp.broadcast_to(tall, square) == wide, iota(square, 0) < iota(square, 1))
    rank = jnp.sum(jnp.where(same, 1.0, 0.0), axis=0, keepdims=True)
    payload = jnp.concatenate([phase, power, got_a[2 * blocks:3 * blocks] + 1.0], axis=1)
    shape = (n_cuts, blocks)
    goes = jnp.broadcast_to(target, shape) == iota(shape, 0).astype(F32)
    for slot in range(2):
        pick = jnp.logical_and(goes, jnp.broadcast_to(rank, shape) == float(slot))
        moved = dot_exact(jnp.where(pick, 1.0, 0.0), payload)
        for part in range(2):
            send_e[pl.ds(slot * 2 + part, n_cuts, stride=8), :] = moved[:, part * width:(part + 1) * width]
        send_x[pl.ds(slot, n_cuts, stride=8), :] = moved[:, 2 * width:]
    carry_cut = jnp.where(jnp.logical_and(g >= n_group - 3, g <= n_group - 2), 1, 0)

    def send_electrons(stage, rows, src, dst):
        for j in cut_order:
            cut = wrap(c + j, n_cuts)
            k = wrap(cut + n_cuts - carry_cut, n_cuts)
            remote(stage, tile(src, k, rows), tile(dst, c, rows), cut, ahead_group).start()

    with tag("sendx"):
        send_electrons(10, 2, send_x, recv_x)

    shape = (n_cuts, n_cuts)
    g_real = g.astype(F32)
    cos, sin = turns((iota(shape, 1).astype(F32) * n_group + g_real) * iota(shape, 0).astype(F32), total)
    cut_fwd[...] = triple(stack2(cos, sin, -sin, cos))
    cos, sin = turns((iota(shape, 0).astype(F32) * n_group + g_real) * iota(shape, 1).astype(F32), total)
    cut_inv[...] = triple(stack2(cos, -sin, sin, cos))
    first_freq = unit // 2
    shape = (n_group, total)
    chosen = iota(shape, 1) == first_freq + n_cuts * iota(shape, 0)
    gain_real = jnp.sum(jnp.where(chosen, jnp.broadcast_to(gain_in[0:1], shape), 0.0), axis=1, keepdims=True)
    gain_imag = jnp.sum(jnp.where(chosen, jnp.broadcast_to(gain_in[1:2], shape), 0.0), axis=1, keepdims=True)
    shape = (n_group, n_group)
    lag_cos, lag_sin = turns((first_freq.astype(F32) + n_cuts * iota(shape, 0).astype(F32)) * 4.0, total)
    scale = 1.0 / total
    turn_real = (gain_real * lag_cos + gain_imag * lag_sin) * scale
    turn_imag = (gain_imag * lag_cos - gain_real * lag_sin) * scale
    cos, sin = turns(iota(shape, 0).astype(F32) * iota(shape, 1).astype(F32), n_group)
    shaped_real = turn_real * cos + turn_imag * sin
    shaped_imag = turn_imag * cos - turn_real * sin
    mid_op[...] = triple(dot_exact(
        stack2(cos, -sin, sin, cos), stack2(shaped_real, -shaped_imag, shaped_imag, shaped_real)
    ))

    def apply(operator, count, source_ref, target_ref):
        real = [source_ref[pl.ds(j, count, stride=8), :] for j in range(HALF)]
        imag = [source_ref[pl.ds(HALF + j, count, stride=8), :] for j in range(HALF)]
        data = jnp.concatenate([jnp.concatenate(real, axis=1), jnp.concatenate(imag, axis=1)], axis=0)
        done = apply_triple(operator[...], data)
        for j in range(HALF):
            target_ref[pl.ds(j, count, stride=8), :] = done[:count, j * grid:(j + 1) * grid]
            target_ref[pl.ds(HALF + j, count, stride=8), :] = done[count:, j * grid:(j + 1) * grid]

    @pl.when(active)
    def _():
        for h in range(2):
            arrived(1 + h, recv1.at[h])
            with tag("fwd%d" % h):
                apply(cut_fwd, n_cuts, recv1.at[h], send2.at[h])
        with tag("send2"):
            for j in quad_order:
                y = wrap(quad + j, quads)
                for r in range(4):
                    src, dst = tile(send2.at[r % 2], 2 * y + r // 2), tile(recv2, g)
                    if j:
                        remote(3, src, dst, c, 4 * y + r).start()
                    else:
                        push(4 * y + r == g, 3, src, dst, c, 4 * y + r)
                low = y - side * (quads // 2)

                @pl.when(jnp.logical_and(low >= 0, low < quads // 2))
                def _():
                    for r in range(4):
                        src = tile(send2.at[r % 2], n_group // 2 + 2 * low + r // 2)
                        remote(3, src, tile(recv2, g), idle_cut, 4 * y + r).start()

    @pl.when(active)
    def _():
        @pl.when(side == g // half_group)
        def _():
            pl.semaphore_signal(go_sem, inc=1, device_id=(idle_cut, g), device_id_type=MESH)

    @pl.when(idle)
    def _():
        with tag("go"):
            pl.semaphore_wait(go_sem, 1)

    with tag("sende"):
        send_electrons(9, 4, send_e, recv_e)

    arrived(3, recv2)
    with tag("mid"):
        apply(mid_op, n_group, recv2, send3)

    for h in range(2):
        @pl.when((unit & 1) == h)
        def _():
            with tag("send3"):
                for j in quad_order:
                    y = wrap(quad + j, quads)
                    for r in range(4):
                        src, dst = tile(send3, 4 * y + r), tile(recv3.at[h], unit >> 1)
                        if j:
                            remote(4 + h, src, dst, owner, 4 * y + r).start()
                        else:
                            push(jnp.logical_and(active, 4 * y + r == g), 4 + h, src, dst, owner, 4 * y + r)

    arrived(10, recv_x.at[pl.ds(0, n_cuts * 2)])

    def cells_of(value):
        return (value + 0.25).astype(jnp.int32) - 1

    cells = jnp.concatenate([recv_x[pl.ds(0, n_cuts, stride=8), :], recv_x[pl.ds(1, n_cuts, stride=8), :]], axis=0)
    slip_p[...] = cells
    remote(11, slip_p, got_p, *device(-1)).start()
    with tag("mark3"):
        alone(lambda: mark(many, cells_of(slip_p[...]), hot_now, row_now, turned_now))

    @pl.when(active)
    def _():
        for h in range(2):
            arrived(4 + h, recv3.at[h])
            with tag("inv%d" % h):
                apply(cut_inv, n_cuts, recv3.at[h], send4.at[h])
        with tag("send4"):
            for j in cut_order:
                cut = wrap(c + j, n_cuts)
                for h in range(2):
                    src, dst = tile(send4.at[h], cut), tile(recv4.at[h], my_active)
                    if j:
                        remote(6 + h, src, dst, cut, g).start()
                    else:
                        keep(6 + h, src, dst)

    arrived(11, got_p)
    with tag("mark4"):
        alone(lambda: mark(many, cells_of(got_p[...]), hot_next, row_next, turned_next))
    arrived(9, recv_e.at[pl.ds(0, n_cuts * 4)])

    def pieces(part):
        return jnp.concatenate(
            [recv_e[pl.ds(part, n_cuts, stride=8), :], recv_e[pl.ds(2 + part, n_cuts, stride=8), :]], axis=0
        )

    phase = pieces(0)
    cos, sin = jnp.cos(phase), jnp.sin(phase)
    for h in range(2):
        arrived(6 + h, recv4.at[h])
        for a in range(n_active):
            at = a * ROWS + h * HALF
            field[at:at + HALF] = recv4[h, a * 8:a * 8 + HALF]
            field[grid + at:grid + at + HALF] = recv4[h, a * 8 + HALF:(a + 1) * 8]

    with tag("look3"):
        alone(lambda: look(many, hot_now, row_now))
    with tag("kick3"):
        phase, power = kick(many, phase, pieces(1), cos, sin)
        slip_b[:many] = phase
        slip_b[many:] = power
    remote(12, slip_b, got_b, *device(-1)).start()
    with tag("deposit3"):
        alone(lambda: deposit(many, row_now, turned_now))
    with tag("diffract3"):
        set_field(diffract(me != 1))

    with tag("look4"):
        alone(lambda: look(many, hot_next, row_next))
    arrived(12, got_b)
    with tag("kick4"):
        phase = got_b[:many]
        kick(many, phase, got_b[many:], jnp.cos(phase), jnp.sin(phase))
    with tag("deposit4"):
        alone(lambda: deposit(many, row_next, turned_next))
    with tag("diffract4"):
        result = diffract(me != 0)
        out[0, 0] = result[:, :grid]
        out[0, 1] = result[:, grid:]

    sent(0, slip_a)
    sent(9, send_e.at[pl.ds(0, n_cuts * 4)])
    sent(10, send_x.at[pl.ds(0, n_cuts * 2)])
    sent(11, slip_p)
    sent(12, slip_b)

    @pl.when(active)
    def _():
        for h in range(2):
            sent(1 + h, send1.at[h, pl.ds(0, (n_active - 1) * 8)])
            sent(6 + h, send4.at[h, pl.ds(0, (n_cuts - 1) * 8)])
        for h in range(2):
            @pl.when((unit & 1) == h)
            def _():
                sent(4 + h, send3.at[pl.ds(0, (n_group - 1) * 8)])
        sent(3, send2.at[0])
        sent(3, send2.at[1, pl.ds(0, (n_cuts - 1) * 8)])

    @pl.when(idle)
    def _():
        for h in range(2):
            sent(1 + h, send1.at[h])
            @pl.when((unit & 1) == h)
            def _():
                sent(4 + h, send3)


def on_device(n_cuts, n_group, radiation, phases, energy, pixels, destination, propagator, transmit):
    grid = radiation.shape[-1]
    blocks, width = phases.shape[1:]
    many = 2 * n_cuts
    n_active = grid // ROWS
    vmem = lambda shape, kind=F32: pltpu.VMEM(shape, kind)
    scratch = [
        vmem((blocks, width)), vmem((blocks, width)), vmem((blocks, width), jnp.int32),
        vmem(destination.shape, jnp.int32), vmem(propagator.shape), vmem(transmit.shape),
        vmem((2 * grid, grid)),
        vmem((2 * grid, 2 * grid), BF16), vmem((2 * grid, 2 * grid), BF16),
        vmem((2 * n_cuts, 6 * n_cuts), BF16), vmem((2 * n_cuts, 6 * n_cuts), BF16),
        vmem((2 * n_group, 6 * n_group), BF16),
        vmem((3 * blocks + 8, width)), vmem((3 * blocks + 8, width)),
        vmem((many, width)), vmem((many, width)),
        vmem((2 * many, width)), vmem((2 * many, width)),
        vmem((2 * grid, many * width), BF16), vmem((2 * grid, many * width), BF16),
        vmem((many * width, 2 * grid), BF16), vmem((many * width, 2 * grid), BF16),
        vmem((many, width), jnp.int32), vmem((many, width), jnp.int32),
        vmem((2, many, width)), vmem((2, many, width)),
        vmem((grid, 2 * grid)),
        vmem((2, n_active * 8, grid)), vmem((2, n_cuts * 8, grid)),
        vmem((2, n_cuts * 8, grid)), vmem((n_group * 8, grid)),
        vmem((n_group * 8, grid)), vmem((2, n_cuts * 8, grid)),
        vmem((2, n_cuts * 8, grid)), vmem((2, n_active * 8, grid)),
        vmem((n_cuts * 8, width)), vmem((n_cuts * 8, width)), vmem((n_cuts * 8, width)), vmem((n_cuts * 8, width)),
        pltpu.SemaphoreType.REGULAR, pltpu.SemaphoreType.DMA((8,)), pltpu.SemaphoreType.DMA((13,)), pltpu.SemaphoreType.DMA((13,)),
    ]
    return pl.pallas_call(
        functools.partial(kernel, n_cuts, n_group, grid, blocks, width),
        out_shape=jax.ShapeDtypeStruct(radiation.shape, F32),
        in_specs=[pl.BlockSpec(memory_space=pltpu.HBM)] * 7,
        out_specs=pl.BlockSpec(memory_space=pltpu.VMEM),
        scratch_shapes=scratch,
        compiler_params=pltpu.CompilerParams(collective_id=0, has_side_effects=True, vmem_limit_bytes=32 << 20),
    )(*(
        pltpu.with_memory_space_constraint(x, pltpu.HBM)
        for x in (radiation, phases, energy, pixels, destination, propagator, transmit)
    ))


def solution(mesh):
    sizes = dict(mesh.shape)
    return jax.shard_map(
        functools.partial(on_device, sizes["cuts"], sizes["group"]),
        mesh=mesh,
        in_specs=(
            P(("cuts", "group"), None, None, None),
            P(("cuts", "group"), None, None),
            P(("cuts", "group"), None, None),
            P(("cuts", "group"), None, None),
            P(("cuts", "group"), None),
            P(),
            P(),
        ),
        out_specs=P(("cuts", "group"), None, None, None),
        check_vma=False,
    )
```
